128 devices in a mesh: lev: 4 (over x), lat: 32 (over y, z, core).
Axes of the slice: x: 4, y: 4, z: 4, core: 2. Of those that a mesh axis runs over, the one named last changes fastest.
Arguments:
- grid_values: bfloat16 [64, 1280, 2560], P(None, 'lat', 'lev'), may hold values from -6 to 6
- basis_table: bfloat16 [640, 640, 1281], P(None, ('lev', 'lat')), may hold values from -6 to 6
- damping_rates: float32 [64], replicated, may hold values from 0.5 to 8
- pair_table: int32 [640], replicated, may hold values from 0 to 639, each once
Outputs:
- coefficients: bfloat16 [160, 4, 2, 64, 1281], P('lat', None, None, 'lev')
The draws below stay inside these ranges and needn't reach their ends.
Inputs may be any that keep to these rules, and one draw needn't show every extreme that they name: `pair_table`: each pair index appears in exactly one slot; the pair p stands for the wavenumbers p and 1279 - p.
All inputs are finite; a program needn't handle non-finite values.
Results may differ from the reference program's by a relative error of at most 0.0062.
Values may be sent and summed in bfloat16 or wider, within the bound.
No kernel may reach another device: no remote copies, remote signals or barrier semaphores. Data moves between devices by JAX's collectives and lax.ppermute only.
A program may use at most 128 MiB of HBM per device.

```python
import math
import jax
import jax.numpy as jnp
from jax import lax

NLON = 2560
NLAT = 1280
WAVES = 1280
LEVELS = 64
PAIRS = 640
N_LEV = 4


def block_scale(key, dims, cuts, low, top_value):
    def one(axis_at, parts):
        draws = jax.random.uniform(jax.random.fold_in(jax.random.fold_in(key, 6), axis_at), (parts,), jnp.float32, low / len(cuts), top_value / len(cuts))
        return jnp.repeat(jnp.exp(draws), dims[axis_at] // parts).reshape((-1,) + (1,) * (len(dims) - axis_at - 1))

    factor_of = one(*cuts[0])
    for cut in cuts[1:]:
        factor_of = factor_of * one(*cut)
    return factor_of


def centred(rng, dims, scale, limit, cuts=(), kind=jnp.bfloat16):
    entries = scale * jax.random.normal(rng, dims, jnp.float32)
    if cuts:
        entries = entries * block_scale(rng, dims, cuts, -0.22, 0.18)
    return jnp.clip(entries, -limit, limit).astype(kind)


def setup_inputs(seed: int = 0) -> dict:
    arg_keys = jax.random.split(jax.random.key(seed), 5)
    return {
        "grid_values": centred(arg_keys[0], (LEVELS, NLAT, NLON), 1.0, 6.0, ((1, 32), (2, 4))),
        "basis_table": centred(arg_keys[1], (NLAT // 2, PAIRS, WAVES + 1), 1.0, 6.0, ((1, 128),)),
        "damping_rates": jnp.clip(jnp.exp(jax.random.uniform(arg_keys[2], (LEVELS,), jnp.float32, math.log(0.5), math.log(8.0))), 0.5, 8.0),
        "pair_table": jax.random.permutation(arg_keys[3], PAIRS).astype(jnp.int32),
    }


def circle_rows(wave_numbers, lon_count):
    longitude = jnp.arange(lon_count, dtype=jnp.int32)
    phase = (wave_numbers[..., None] * longitude) % lon_count
    angle = phase.astype(jnp.float32) * (2.0 * math.pi / lon_count)
    return jnp.stack([jnp.cos(angle), -jnp.sin(angle)], axis=-2).astype(jnp.bfloat16)


def reference(grid_values, basis_table, damping_rates, pair_table):
    top_wave = WAVES - 1
    circle = circle_rows(jnp.arange(WAVES, dtype=jnp.int32), NLON).reshape(2 * WAVES, NLON)
    circle_cols = circle.T

    def transform(level_rows):
        widened = level_rows.astype(jnp.float32)
        squared = (widened * jnp.abs(widened)).astype(jnp.bfloat16)
        spectra = jnp.dot(squared, circle_cols, preferred_element_type=jnp.float32)
        return (spectra * (1.0 / NLON)).astype(jnp.bfloat16)

    fourier = lax.map(transform, grid_values)
    half_lats = NLAT // 2
    north_rows = fourier[:, :half_lats]
    south_rows = fourier[:, ::-1][:, :half_lats]
    member_waves = jnp.stack([pair_table, top_wave - pair_table], axis=1)
    col_index = (member_waves[:, :, None] * 2 + jnp.arange(2, dtype=jnp.int32)).reshape(-1).astype(jnp.int32)
    north_cols = jnp.take(north_rows, col_index, axis=2).reshape(LEVELS, half_lats, PAIRS, 2, 2)
    south_cols = jnp.take(south_rows, col_index, axis=2).reshape(LEVELS, half_lats, PAIRS, 2, 2)
    column_ids = jnp.arange(WAVES + 1, dtype=jnp.int32)

    def one_pair(slot):
        pair_value = pair_table[slot]
        basis_slot = lax.dynamic_index_in_dim(basis_table, slot, 1, keepdims=False)
        north_slot = lax.dynamic_index_in_dim(north_cols, slot, 2, keepdims=False)
        south_slot = lax.dynamic_index_in_dim(south_cols, slot, 2, keepdims=False)
        north_flat = jnp.transpose(north_slot, (2, 3, 0, 1)).reshape(4 * LEVELS, half_lats)
        south_flat = jnp.transpose(south_slot, (2, 3, 0, 1)).reshape(4 * LEVELS, half_lats)
        north_prod = jnp.dot(north_flat, basis_slot, preferred_element_type=jnp.float32).reshape(2, 2, LEVELS, WAVES + 1)
        south_prod = jnp.dot(south_flat, basis_slot, preferred_element_type=jnp.float32).reshape(2, 2, LEVELS, WAVES + 1)
        second_member = column_ids >= WAVES - pair_value
        degree = jnp.where(second_member, column_ids - 1, pair_value + column_ids)
        order_m = jnp.where(second_member, top_wave - pair_value, pair_value)
        parity_sign = jnp.where((degree - order_m) % 2 == 0, 1.0, -1.0).astype(jnp.float32)
        scaled = (degree * (degree + 1)).astype(jnp.float32) / float(top_wave * (top_wave + 1))
        north_pick = jnp.where(second_member, north_prod[1], north_prod[0])
        south_pick = jnp.where(second_member, south_prod[1], south_prod[0])
        combined = north_pick + parity_sign * south_pick
        factor = 1.0 / (1.0 + damping_rates[:, None] * (scaled * scaled)[None, :])
        return (combined * factor).astype(jnp.bfloat16)

    spectral = lax.map(one_pair, jnp.arange(PAIRS, dtype=jnp.int32))
    spectral = spectral.reshape(N_LEV, PAIRS // N_LEV, 2, LEVELS, WAVES + 1)
    return jnp.transpose(spectral, (1, 0, 2, 3, 4))
```

```python
import functools
import math

import jax
import jax.numpy as jnp
import numpy as np
from jax import lax
from jax.experimental import pallas as pl
from jax.experimental.pallas import tpu as pltpu
from jax.sharding import PartitionSpec as P

F32 = jnp.float32
BF16 = jnp.bfloat16
NT = (((1,), (1,)), ((), ()))
NN = (((1,), (0,)), ((), ()))
LANES = 128
VMEM_BYTES = 60 * 1024 * 1024


COS_TERMS = [((-1) ** n) * (2 * math.pi) ** (2 * n) / math.factorial(2 * n) for n in range(10)]


def cos_turns(turns):
    part = turns - jnp.floor(turns + 0.5)
    square = part * part
    total = jnp.full_like(square, COS_TERMS[-1])
    for term in COS_TERMS[-2::-1]:
        total = total * square + term
    return total


def circle_kernel(lon_count, wave_ref, quarter_ref, out_ref):
    rows, cols = out_ref.shape
    wave = wave_ref[...].astype(F32)
    quarter = quarter_ref[...].astype(F32) * 0.25
    lane = lax.broadcasted_iota(jnp.int32, (rows, LANES), 1).astype(F32)

    def at(offset):
        product = wave * (lane + offset)
        product = product - jnp.floor(product * (1.0 / lon_count)) * lon_count
        return cos_turns(product * (1.0 / lon_count) + quarter)

    step = wave * float(LANES)
    step = step - jnp.floor(step * (1.0 / lon_count)) * lon_count
    twice = 2.0 * cos_turns(step * (1.0 / lon_count))
    before, now = at(0.0), at(float(LANES))
    out_ref[:, :LANES] = before.astype(BF16)
    out_ref[:, LANES : 2 * LANES] = now.astype(BF16)
    for tile in range(2, cols // LANES):
        before, now = now, twice * now - before
        out_ref[:, tile * LANES : (tile + 1) * LANES] = now.astype(BF16)


def circle_table(waves, quarters, lon_count, cols):
    rows = waves.shape[0]
    block = 64
    spread = lambda v: jnp.broadcast_to(v[:, None], (rows, LANES))
    return pl.pallas_call(
        functools.partial(circle_kernel, lon_count),
        grid=(rows // block,),
        in_specs=[pl.BlockSpec((block, LANES), lambda i: (i, 0))] * 2,
        out_specs=pl.BlockSpec((block, cols), lambda i: (i, 0)),
        out_shape=jax.ShapeDtypeStruct((rows, cols), BF16),
        cost_estimate=pl.CostEstimate(
            flops=rows * cols * 10, bytes_accessed=rows * cols * 2, transcendentals=0
        ),
        name="circle",
    )(spread(waves), spread(quarters))


def fourier_kernel(south_ref, g_ref, circle_ref, spread_ref, lane_ref, out_ref, fold_ref):
    dests = out_ref.shape[0]
    quarter = g_ref.shape[2]
    lats = g_ref.shape[1]
    bands = g_ref.shape[0] // 4
    tiles = bands * lats // LANES
    main = dests * 8

    @pl.when(pl.program_id(0) == 0)
    def _():
        def step(b, carry):
            def squared(q):
                value = g_ref[pl.ds(q * bands + 2 * b, 2)].astype(F32)
                return (value * jnp.abs(value)).reshape(2 * lats, quarter)

            rows = pl.ds(pl.multiple_of(b * 2 * lats, 16), 2 * lats)
            for half in range(2):
                near, far = squared(half), squared(half + 2)
                cols = slice(half * quarter, (half + 1) * quarter)
                fold_ref[0, rows, cols] = (near + far).astype(BF16)
                fold_ref[1, rows, cols] = (near - far).astype(BF16)
            return carry

        lax.fori_loop(0, bands // 2, step, 0)

    south = south_ref[0]
    pieces = []
    for tile in range(tiles):
        rows = slice(tile * LANES, (tile + 1) * LANES)
        both = []
        for kind in range(2):
            value = lax.dot_general(
                circle_ref[0, kind], fold_ref[kind, rows, :], NT, preferred_element_type=F32
            )
            index = jnp.broadcast_to(lane_ref[0:1, :], value.shape)
            value = jnp.take_along_axis(value, index, axis=1, mode="promise_in_bounds")
            both.append(value[:main].reshape(dests, 8, LANES))
            pieces.append(value[main:].astype(BF16))
        place = jnp.where(south == 1, tiles - 1 - tile, tile)
        out_ref[:, pl.ds(pl.multiple_of(place * 16, 16), 16), :] = jnp.concatenate(
            both, axis=1
        ).astype(BF16)
    last = jnp.concatenate(pieces, axis=0)
    moved = lax.dot_general(spread_ref[...], last, NN, preferred_element_type=F32)
    out_ref[:, tiles * 16 :, :] = moved.reshape(dests, 24, LANES).astype(BF16)


def fourier(south, received, circle, spread, lane_index, dev_count):
    steps = circle.shape[0]
    dests = dev_count // steps
    bands4, lats, quarter = received.shape
    lat_half = bands4 // 4 * lats
    tiles = lat_half // LANES
    rows = tiles * 16 + 24
    return pl.pallas_call(
        fourier_kernel,
        grid_spec=pltpu.PrefetchScalarGridSpec(
            num_scalar_prefetch=1,
            grid=(steps,),
            in_specs=[
                pl.BlockSpec(received.shape, lambda i, s: (0, 0, 0)),
                pl.BlockSpec((1,) + circle.shape[1:], lambda i, s: (i, 0, 0, 0)),
                pl.BlockSpec(spread.shape, lambda i, s: (0, 0)),
                pl.BlockSpec(lane_index.shape, lambda i, s: (0, 0)),
            ],
            out_specs=pl.BlockSpec((dests, rows, LANES), lambda i, s: (i, 0, 0)),
            scratch_shapes=[pltpu.VMEM((2, lat_half, 2 * quarter), BF16)],
        ),
        out_shape=jax.ShapeDtypeStruct((dev_count, rows, LANES), BF16),
        compiler_params=pltpu.CompilerParams(vmem_limit_bytes=VMEM_BYTES),
        name="fourier",
    )(south, received, circle, spread, lane_index)


def legendre_kernel(
    scale, norm, pairs_ref, recv_ref, basis_ref, rate_ref, mix_ref, tail_ref, last_ref, out_ref, x_ref
):
    slot = pl.program_id(0)
    levs = out_ref.shape[0]
    cols = basis_ref.shape[1]
    waves = cols - 1
    lat_half = basis_ref.shape[2]
    tiles = lat_half // LANES
    group = recv_ref.shape[0] // (2 * levs)

    @pl.when(slot == 0)
    def _():
        def step(x, carry):
            north = pl.ds(x * 2 * group, group)
            south = pl.ds(x * 2 * group + group, group)
            dest = pl.ds(pl.multiple_of(x * 32, 32), 32)

            def moved(rows, height, matrix):
                n = recv_ref[north, rows, :].reshape(group * height, LANES).astype(F32)
                s = recv_ref[south, rows, :].reshape(group * height, LANES).astype(F32)
                sides = jnp.concatenate([n + s, n - s], axis=1).astype(BF16)
                return lax.dot_general(
                    matrix, sides, NN, preferred_element_type=F32
                ).astype(BF16)

            for tile in range(tiles):
                value = moved(slice(tile * 16, tile * 16 + 16), 16, mix_ref[...])
                lanes = slice(tile * LANES, (tile + 1) * LANES)
                for k in range(4):
                    for kind in range(2):
                        part = value[(k * 2 + kind) * 32 : (k * 2 + kind + 1) * 32]
                        for par in range(2):
                            x_ref[k, par, kind, dest, lanes] = part[:, par * LANES : (par + 1) * LANES]
            base = tiles * 16
            value = moved(slice(base, base + 16), 16, tail_ref[...])
            end = moved(slice(base + 16, base + 24), 8, last_ref[...])
            for tile in range(tiles):
                lanes = slice(tile * LANES, (tile + 1) * LANES)
                for kind in range(2):
                    part = (
                        value[(tile * 2 + kind) * 32 : (tile * 2 + kind + 1) * 32]
                        if tile < 4
                        else end[kind * 32 : (kind + 1) * 32]
                    )
                    for par in range(2):
                        x_ref[4, par, kind, dest, lanes] = part[:, par * LANES : (par + 1) * LANES]
            return carry

        lax.fori_loop(0, levs, step, 0)

    pair = pairs_ref[slot]
    bound = waves - pair
    first_kind = lax.rem(pair, 2)
    rate = rate_ref[...]
    rows = levs * 32

    def damping(column, second):
        degree = jnp.where(second, column - 1, pair + column)
        scaled = (degree * (degree + 1)).astype(F32) / norm
        return scale / (1.0 + rate[:, : column.shape[1]] * (scaled * scaled))

    width = 256

    def block(start):
        column = start + lax.broadcasted_iota(jnp.int32, (1, width), 1)
        second = column >= bound
        even = lax.rem(jnp.where(second, column + pair, column), 2) == 0
        factor = damping(column, second)
        basis = basis_ref[0, start : start + width, :]

        def product(kind):
            left = x_ref[slot, :, kind].reshape(2 * rows, lat_half)
            both = lax.dot_general(left, basis, NT, preferred_element_type=F32)
            return jnp.where(even, both[:rows], both[rows:])

        whole = start >= bound
        value = product(jnp.where(whole, 1 - first_kind, first_kind)) * factor
        out_ref[:, 0, :, start : start + width] = value.astype(BF16).reshape(levs, 32, width)

        @pl.when((start < bound) & (bound < start + width))
        def _():
            other = product(1 - first_kind) * factor
            kept = jnp.where(second, other, value)
            out_ref[:, 0, :, start : start + width] = kept.astype(BF16).reshape(levs, 32, width)

    for start in range(0, waves, width):
        block(start)
    column = jnp.full((1, 1), waves, jnp.int32)
    left = x_ref[slot, first_kind, 1 - first_kind].astype(F32)
    final = jnp.sum(left * basis_ref[0, waves:cols, :].astype(F32), axis=1, keepdims=True)
    final = final * damping(column, column >= bound)
    out_ref[:, 0, :, waves:cols] = final.astype(BF16).reshape(levs, 32, 1)


def legendre(pairs, received, basis, rates, mix, tail, last, levs, lon_count, norm):
    slots, cols, lat_half = basis.shape
    whole = lambda a: pl.BlockSpec(a.shape, lambda k, p: (0,) * a.ndim)
    return pl.pallas_call(
        functools.partial(legendre_kernel, 1.0 / lon_count, norm),
        grid_spec=pltpu.PrefetchScalarGridSpec(
            num_scalar_prefetch=1,
            grid=(slots,),
            in_specs=[
                whole(received),
                pl.BlockSpec((1, cols, lat_half), lambda k, p: (k, 0, 0)),
                whole(rates),
                whole(mix),
                whole(tail),
                whole(last),
            ],
            out_specs=pl.BlockSpec((levs, 1, 32, cols), lambda k, p: (0, k, 0, 0)),
            scratch_shapes=[pltpu.VMEM((slots, 2, 2, levs * 32, lat_half), BF16)],
        ),
        out_shape=jax.ShapeDtypeStruct((levs, slots, 32, cols), BF16),
        compiler_params=pltpu.CompilerParams(vmem_limit_bytes=VMEM_BYTES),
        name="legendre",
    )(pairs, received, basis, rates, mix, tail, last)


def placing(out_rows, in_rows, target):
    goal = target(lax.broadcasted_iota(jnp.int32, (out_rows, in_rows), 1))
    return (goal == lax.broadcasted_iota(jnp.int32, (out_rows, in_rows), 0)).astype(BF16)


def per_device(grid_values, basis_table, damping_rates, pair_table):
    levs, lat_count = lax.axis_size("lev"), lax.axis_size("lat")
    dev_count = levs * lat_count
    half_bands = lat_count // 2
    lon_count = grid_values.shape[2] * levs
    slots, cols = basis_table.shape[1], basis_table.shape[2]
    top = cols - 2
    lat_half = basis_table.shape[0]
    tiles = lat_half // LANES
    group = half_bands
    me_lat = lax.axis_index("lat")
    flat = lax.axis_index("lev") * lat_count + me_lat
    south = (me_lat >= half_bands).astype(jnp.int32)

    groups = [
        [x * lat_count + h * half_bands + b for x in range(levs) for b in range(half_bands)]
        for h in range(2)
    ]
    circles = lax.all_to_all(
        grid_values, ("lev", "lat"), 0, 0, axis_index_groups=groups, tiled=True
    )

    steps = 4
    other = top - pair_table
    odd = pair_table % 2 == 1
    kinds = []
    for wave in (jnp.where(odd, other, pair_table), jnp.where(odd, pair_table, other)):
        wave = jnp.repeat(wave.reshape(steps, dev_count // steps, slots), 2, axis=2)
        head = wave[:, :, : 2 * slots - 2].reshape(steps, -1)
        kinds.append(jnp.concatenate([head, wave[:, :, 2 * slots - 2 :].reshape(steps, -1)], axis=1))
    waves = jnp.stack(kinds, axis=1)
    quarters = jnp.broadcast_to(jnp.arange(waves.shape[2], dtype=jnp.int32) % 2, waves.shape)
    circle = circle_table(
        waves.reshape(-1), quarters.reshape(-1), lon_count, lon_count // 2
    ).reshape(waves.shape + (lon_count // 2,))

    dests = dev_count // steps
    count = dests * 2

    def spread_target(i):
        tile, rest = i // (2 * count), i % (2 * count)
        kind, rest = rest // count, rest % count
        tile = jnp.where(south == 1, tiles - 1 - tile, tile)
        return (rest // 2) * 24 + tile * 4 + kind * 2 + rest % 2

    spread = placing(dests * 24, tiles * 2 * count, spread_target)
    lane = jnp.arange(LANES, dtype=jnp.int32)
    lane_index = jnp.broadcast_to(jnp.where(south == 1, LANES - 1 - lane, lane), (8, LANES))
    packed = fourier(south[None], circles, circle, spread, lane_index, dev_count)
    received = lax.all_to_all(packed, ("lev", "lat"), 0, 0, tiled=True)

    def mix_target(i):
        level, row = i // 16, i % 16
        kind, k, r = row // 8, row // 2 % 4, row % 2
        return ((k * 2 + kind) * 2 + r) * group + level

    def tail_target(i):
        level, row = i // 16, i % 16
        return row * group + level

    def last_target(i):
        level, row = i // 8, i % 8
        return row * group + level

    mix = placing(256, 256, mix_target)
    tail = placing(256, 256, tail_target)
    last = placing(64, 128, last_target)
    pairs = lax.dynamic_slice_in_dim(pair_table, flat * slots, slots)
    rates = jnp.broadcast_to(damping_rates.reshape(levs, 1, group), (levs, 2, group)).reshape(-1)
    rates = jnp.broadcast_to(rates[:, None], (rates.shape[0], 256))
    outgoing = legendre(
        pairs,
        received,
        jnp.transpose(basis_table, (1, 2, 0)),
        rates,
        mix,
        tail,
        last,
        levs,
        lon_count,
        float(top * (top + 1)),
    )
    result = lax.all_to_all(outgoing, "lev", 0, 0, tiled=True)
    return jnp.transpose(result, (1, 0, 2, 3)).reshape(slots, levs, 2, group, cols)


def solution(mesh):
    placed = (P(None, "lat", "lev"), P(None, ("lev", "lat"), None), P(), P())
    return jax.shard_map(
        per_device,
        mesh=mesh,
        in_specs=placed,
        out_specs=P("lat", None, None, "lev", None),
        check_vma=False,
    )
```

```python
import functools
import math

import jax
import jax.numpy as jnp
from jax import lax
from jax.experimental import pallas as pl
from jax.experimental.pallas import tpu as pltpu
from jax.sharding import PartitionSpec as P


F32 = jnp.float32
BF16 = jnp.bfloat16
NT = (((1,), (1,)), ((), ()))
LANES = 128


COS_TERMS = [((-1) ** n) * (2 * math.pi) ** (2 * n) / math.factorial(2 * n) for n in range(10)]


def cos_turns(turns):
    part = turns - jnp.floor(turns + 0.5)
    square = part * part
    total = jnp.full_like(square, COS_TERMS[-1])
    for term in COS_TERMS[-2::-1]:
        total = total * square + term
    return total


def circle_kernel(lon_count, wave_ref, quarter_ref, out_ref):
    rows, cols = out_ref.shape
    wave = wave_ref[...].astype(F32)
    quarter = quarter_ref[...].astype(F32) * 0.25
    lane = lax.broadcasted_iota(jnp.int32, (rows, LANES), 1).astype(F32)

    def at(offset):
        product = wave * (lane + offset)
        product = product - jnp.floor(product * (1.0 / lon_count)) * lon_count
        return cos_turns(product * (1.0 / lon_count) + quarter)

    step = wave * float(LANES)
    step = step - jnp.floor(step * (1.0 / lon_count)) * lon_count
    twice = 2.0 * cos_turns(step * (1.0 / lon_count))
    before, now = at(0.0), at(float(LANES))
    out_ref[:, :LANES] = before.astype(BF16)
    out_ref[:, LANES : 2 * LANES] = now.astype(BF16)
    for tile in range(2, cols // LANES):
        before, now = now, twice * now - before
        out_ref[:, tile * LANES : (tile + 1) * LANES] = now.astype(BF16)


def circle_table(waves, quarters, lon_count, cols):
    rows = waves.shape[0]
    block = 64
    spread = lambda v: jnp.broadcast_to(v[:, None], (rows, LANES))
    return pl.pallas_call(
        functools.partial(circle_kernel, lon_count),
        grid=(rows // block,),
        in_specs=[pl.BlockSpec((block, LANES), lambda i: (i, 0))] * 2,
        out_specs=pl.BlockSpec((block, cols), lambda i: (i, 0)),
        out_shape=jax.ShapeDtypeStruct((rows, cols), BF16),
        cost_estimate=pl.CostEstimate(
            flops=rows * cols * 10, bytes_accessed=rows * cols * 2, transcendentals=0
        ),
        name="circle",
    )(spread(waves), spread(quarters))


def fourier_kernel(
    south_ref, g_ref, circle_ref, lane_ref, out_ref, g_buf, circle_buf, fold_ref, tail_ref, out_buf,
    g_sem, circle_sem, out_sem,
):
    steps, dests = out_buf.shape[:2]
    _, bands, lats, quarter = g_buf.shape
    tiles = bands * lats // LANES
    main = dests * 8
    end = out_ref.shape[1] - tiles * 16
    groups = [(low, min(2, tiles - low)) for low in range(0, tiles, 2)]
    south = south_ref[0]

    def g_copy(j):
        part = pl.ds(2 * j, 2)
        return pltpu.make_async_copy(g_ref.at[:, part], g_buf.at[:, part], g_sem.at[j])

    def circle_copy(i):
        return pltpu.make_async_copy(circle_ref.at[i], circle_buf.at[i], circle_sem.at[i])

    for j in range(bands // 2):
        g_copy(j).start()
    for i in range(steps):
        circle_copy(i).start()
    tail_ref[...] = jnp.zeros_like(tail_ref)

    def fold(j, carry):
        g_copy(j).wait()

        def squared(q):
            value = g_buf[q, pl.ds(2 * j, 2)].astype(F32)
            return (value * jnp.abs(value)).reshape(2 * lats, quarter)

        rows = pl.ds(pl.multiple_of(j * 2 * lats, 16), 2 * lats)
        for half in range(2):
            near, far = squared(half), squared(half + 2)
            cols = slice(half * quarter, (half + 1) * quarter)
            fold_ref[0, rows, cols] = (near + far).astype(BF16)
            fold_ref[1, rows, cols] = (near - far).astype(BF16)
        return carry

    lax.fori_loop(0, bands // 2, fold, 0)
    index = jnp.broadcast_to(lane_ref[0:1, :], (circle_buf.shape[2], LANES))

    def out_copy(i, start, size, sem):
        rows = pl.ds(start, size)
        return pltpu.make_async_copy(
            out_buf.at[i, :, rows], out_ref.at[pl.ds(i * dests, dests), rows], out_sem.at[i, sem]
        )

    def start_of(low, many):
        start = jnp.where(south == 1, tiles - low - many, low) * 16
        return pl.multiple_of(start, 16)

    def step(i, carry):
        circle_copy(i).wait()
        for n, (low, many) in enumerate(groups):
            rows = slice(low * LANES, (low + many) * LANES)
            values = [
                lax.dot_general(
                    circle_buf[i, kind], fold_ref[kind, rows, :], NT, preferred_element_type=F32
                )
                for kind in range(2)
            ]
            for at in range(many):
                place = jnp.where(south == 1, tiles - 1 - (low + at), low + at)
                both = []
                for kind in range(2):
                    value = jnp.take_along_axis(
                        values[kind][:, at * LANES : (at + 1) * LANES],
                        index,
                        axis=1,
                        mode="promise_in_bounds",
                    )
                    both.append(value[:main].reshape(dests, 8, LANES))
                    for r in range(2):
                        spot = pl.ds(place * 4 + kind * 2 + r, dests, stride=end)
                        tail_ref[spot, :] = value[main + r * dests : main + (r + 1) * dests]
                rows16 = pl.ds(pl.multiple_of(place * 16, 16), 16)
                out_buf[i, :, rows16, :] = jnp.concatenate(both, axis=1).astype(BF16)
            out_copy(i, start_of(low, many), many * 16, n).start()
        last = tail_ref[...].reshape(dests, end, LANES)
        out_buf[i, :, tiles * 16 :, :] = last.astype(BF16)
        out_copy(i, tiles * 16, end, len(groups)).start()
        return carry

    lax.fori_loop(0, steps, step, 0)
    for i in range(steps):
        for n, (low, many) in enumerate(groups):
            out_copy(i, start_of(low, many), many * 16, n).wait()
        out_copy(i, tiles * 16, end, len(groups)).wait()


def fourier(south, received, circle, lane_index, dev_count):
    steps = circle.shape[0]
    dests = dev_count // steps
    _, bands, lats, quarter = received.shape
    lat_half = bands * lats
    tiles = lat_half // LANES
    end = -(-tiles * 4 // 8) * 8
    rows = tiles * 16 + end
    anywhere = pl.BlockSpec(memory_space=pl.ANY)
    return pl.pallas_call(
        fourier_kernel,
        in_specs=[
            pl.BlockSpec(memory_space=pltpu.SMEM),
            anywhere,
            pl.BlockSpec(memory_space=pltpu.HBM),
            pl.BlockSpec(memory_space=pltpu.VMEM),
        ],
        out_specs=pl.BlockSpec(memory_space=pltpu.HBM),
        scratch_shapes=[
            pltpu.VMEM(received.shape, BF16),
            pltpu.VMEM(circle.shape, BF16),
            pltpu.VMEM((2, lat_half, 2 * quarter), BF16),
            pltpu.VMEM((dests * end, LANES), F32),
            pltpu.VMEM((steps, dests, rows, LANES), BF16),
            pltpu.SemaphoreType.DMA((bands // 2,)),
            pltpu.SemaphoreType.DMA((steps,)),
            pltpu.SemaphoreType.DMA((steps, -(-tiles // 2) + 1)),
        ],
        out_shape=jax.ShapeDtypeStruct((dev_count, rows, LANES), BF16),
        compiler_params=pltpu.CompilerParams(vmem_limit_bytes=FOURIER_VMEM),
        cost_estimate=pl.CostEstimate(
            flops=2 * circle.size * lat_half,
            bytes_accessed=2 * (received.size + circle.size + dev_count * rows * LANES),
            transcendentals=0,
        ),
        name="fourier",
    )(south, received, circle, lane_index)


FOURIER_VMEM = 59 * 1024 * 1024
LEGENDRE_VMEM = 113 * 512 * 1024


def legendre_kernel(
    scale, norm, first, count, me_ref, pairs_ref, recv_ref, basis_ref, rate_ref, *refs
):
    levs = recv_ref.shape[1]
    out_refs = refs[:levs]
    recv_buf, basis_buf, x_ref, main_ref, tail_ref, out_buf, recv_sem, basis_sem, out_sem = refs[levs:]
    group = recv_ref.shape[0] // 2
    cols, lats = basis_ref.shape[1:]
    waves = cols - 1
    tiles = lats // LANES
    end = recv_ref.shape[2] - tiles * 16
    rows = x_ref.shape[3]
    part = rows // levs
    me = me_ref[0]

    def recv_copy(x):
        return pltpu.make_async_copy(recv_ref.at[:, x], recv_buf.at[x], recv_sem.at[x])

    def basis_copy(k):
        return pltpu.make_async_copy(basis_ref.at[first + k], basis_buf.at[k], basis_sem.at[k])

    for x in range(levs):
        recv_copy(x).start()
    for k in range(count):
        basis_copy(k).start()

    mains = [k for k in range(first, first + count) if k < 4]

    def gather(x, carry):
        recv_copy(x).wait()
        base = lax.rem(x - me + levs, levs) * part

        def sides(span, height, into):
            n = recv_buf[x, :group, span, :].astype(F32).reshape(group * height, LANES)
            s = recv_buf[x, group:, span, :].astype(F32).reshape(group * height, LANES)
            into[0] = n + s
            into[1] = n - s

        def put(slot, kind, tile, r, from_ref, start, stride):
            lanes = slice(tile * LANES, (tile + 1) * LANES)
            dest = pl.ds(pl.multiple_of(base + r * group, 16), group)
            for par in range(2):
                value = from_ref[par, pl.ds(start, group, stride=stride), :]
                x_ref[slot - first, par, kind, dest, lanes] = value.astype(BF16)

        for tile in range(tiles):
            sides(slice(tile * 16, tile * 16 + 16), 16, main_ref.at[tile])
            for kind in range(2):
                for k in mains:
                    for r in range(2):
                        put(k, kind, tile, r, main_ref.at[tile], kind * 8 + k * 2 + r, 16)
        if first + count > 4:
            sides(slice(tiles * 16, tiles * 16 + end), end, tail_ref)
            for tile in range(tiles):
                for kind in range(2):
                    for r in range(2):
                        put(4, kind, tile, r, tail_ref, tile * 4 + kind * 2 + r, end)
        return carry

    lax.fori_loop(0, levs, gather, 0)

    width = 256
    rate = jnp.broadcast_to(rate_ref[...], (rows, LANES))
    rates = jnp.concatenate([rate] * (width // LANES), axis=1)

    def out_copy(k, s):
        return pltpu.make_async_copy(out_buf.at[s, k], out_refs[s].at[k], out_sem.at[k, s])

    def slot_step(k, carry):
        basis_copy(k).wait()
        pair = pairs_ref[k + first]
        bound = waves - pair
        first_kind = lax.rem(pair, 2)

        def damping(column, second):
            degree = jnp.where(second, column - 1, pair + column)
            scaled = (degree * (degree + 1)).astype(F32) / norm
            return scale / (1.0 + rates[:, : column.shape[1]] * (scaled * scaled))

        def emit(start, value):
            value = value.astype(BF16)
            for s in range(levs):
                out_buf[s, k, :, start : start + value.shape[1]] = value[s * part : (s + 1) * part]

        def block(start):
            column = start + lax.broadcasted_iota(jnp.int32, (1, width), 1)
            second = column >= bound
            even = lax.rem(jnp.where(second, column + pair, column), 2) == 0
            factor = damping(column, second)
            basis = basis_buf[k, start : start + width, :]

            def product(kind):
                left = x_ref[k, :, kind].reshape(2 * rows, lats)
                both = lax.dot_general(left, basis, NT, preferred_element_type=F32)
                return jnp.where(even, both[:rows], both[rows:]) * factor

            value = product(jnp.where(start >= bound, 1 - first_kind, first_kind))
            emit(start, value)

            @pl.when((start < bound) & (bound < start + width))
            def _():
                emit(start, jnp.where(second, product(1 - first_kind), value))

        for start in range(0, waves, width):
            block(start)
        column = jnp.full((1, 1), waves, jnp.int32)
        left = x_ref[k, first_kind, 1 - first_kind].astype(F32)
        final = jnp.sum(left * basis_buf[k, waves:, :].astype(F32), axis=1, keepdims=True)
        emit(waves, final * damping(column, column >= bound))
        for s in range(levs):
            out_copy(k, s).start()
        return carry

    lax.fori_loop(0, count, slot_step, 0)
    for k in range(count):
        for s in range(levs):
            out_copy(k, s).wait()


def legendre(first, count, me, pairs, received, basis, rates, lon_count, norm):
    _, cols, lats = basis.shape
    lat_count, levs, rows, _ = received.shape
    group = lat_count // 2
    part = 2 * group
    tiles = lats // LANES
    end = rows - tiles * 16
    anywhere = pl.BlockSpec(memory_space=pl.ANY)
    scalars = pl.BlockSpec(memory_space=pltpu.SMEM)
    return pl.pallas_call(
        functools.partial(legendre_kernel, 1.0 / lon_count, norm, first, count),
        in_specs=[
            scalars,
            scalars,
            anywhere,
            pl.BlockSpec(memory_space=pltpu.HBM),
            pl.BlockSpec(memory_space=pltpu.VMEM),
        ],
        out_specs=[anywhere] * levs,
        scratch_shapes=[
            pltpu.VMEM((levs, lat_count, rows, LANES), BF16),
            pltpu.VMEM((count, cols, lats), BF16),
            pltpu.VMEM((count, 2, 2, levs * part, lats), BF16),
            pltpu.VMEM((tiles, 2, group * 16, LANES), F32),
            pltpu.VMEM((2, group * end, LANES), F32),
            pltpu.VMEM((levs, count, part, cols), BF16),
            pltpu.SemaphoreType.DMA((levs,)),
            pltpu.SemaphoreType.DMA((count,)),
            pltpu.SemaphoreType.DMA((count, levs)),
        ],
        out_shape=[jax.ShapeDtypeStruct((count, part, cols), BF16)] * levs,
        compiler_params=pltpu.CompilerParams(vmem_limit_bytes=LEGENDRE_VMEM),
        cost_estimate=pl.CostEstimate(
            flops=2 * count * cols * lats * 256,
            bytes_accessed=2 * count * cols * (lats + 128),
            transcendentals=0,
        ),
        name="legendre",
    )(me, pairs, received, basis, rates)


def assemble_kernel(counts, me_ref, *refs):
    levs = refs[-2].shape[1]
    out_ref, sem = refs[-2:]
    copies, low = [], 0
    for c, count in enumerate(counts):
        for s in range(levs):
            lev = lax.rem(me_ref[0] - s + levs, levs)
            n = c * levs + s
            dest = out_ref.at[low : low + count, lev]
            copies.append(pltpu.make_async_copy(refs[n], dest, sem.at[n]))
        low += count
    for copy in copies:
        copy.start()
    for copy in copies:
        copy.wait()


def assemble(me, parts):
    levs = len(parts[0])
    _, part, cols = parts[0][0].shape
    counts = [p[0].shape[0] for p in parts]
    flat = [a for p in parts for a in p]
    anywhere = pl.BlockSpec(memory_space=pl.ANY)
    return pl.pallas_call(
        functools.partial(assemble_kernel, counts),
        in_specs=[pl.BlockSpec(memory_space=pltpu.SMEM)] + [anywhere] * len(flat),
        out_specs=anywhere,
        scratch_shapes=[pltpu.SemaphoreType.DMA((len(flat),))],
        out_shape=jax.ShapeDtypeStruct((sum(counts), levs, part, cols), BF16),
        compiler_params=pltpu.CompilerParams(vmem_limit_bytes=1024 * 1024),
        name="assemble",
    )(me, *flat)


def transform(grid_values, basis_table, damping_rates, pair_table):
    levs, lat_count = lax.axis_size("lev"), lax.axis_size("lat")
    dev_count = levs * lat_count
    half_bands = lat_count // 2
    lon_count = grid_values.shape[2] * levs
    slots, cols = basis_table.shape[1], basis_table.shape[2]
    top = cols - 2
    group = half_bands
    me_lev, me_lat = lax.axis_index("lev"), lax.axis_index("lat")
    south = (me_lat >= half_bands).astype(jnp.int32)

    halves = [
        [x * lat_count + h * half_bands + b for x in range(levs) for b in range(half_bands)]
        for h in range(2)
    ]
    everyone = [[x * lat_count + b for b in range(lat_count) for x in range(levs)]]
    circles = lax.all_to_all(
        grid_values, ("lev", "lat"), 0, 0, axis_index_groups=halves, tiled=True
    ).reshape((levs, half_bands) + grid_values.shape[1:])

    steps = 2
    table = jnp.transpose(pair_table.reshape(levs, lat_count, slots), (1, 0, 2))
    table = table.reshape(steps, dev_count // steps, slots)
    other = top - table
    odd = table % 2 == 1
    kinds = []
    for wave in (jnp.where(odd, other, table), jnp.where(odd, table, other)):
        head = jnp.repeat(wave[:, :, : slots - 1], 2, axis=2).reshape(steps, -1)
        kinds.append(jnp.concatenate([head, wave[:, :, slots - 1], wave[:, :, slots - 1]], axis=1))
    waves = jnp.stack(kinds, axis=1)
    row = jnp.arange(waves.shape[2], dtype=jnp.int32)
    main = dev_count // steps * 2 * (slots - 1)
    quarters = jnp.where(row < main, row % 2, (row >= main + dev_count // steps).astype(jnp.int32))
    quarters = jnp.broadcast_to(quarters, waves.shape)
    circle = circle_table(
        waves.reshape(-1), quarters.reshape(-1), lon_count, lon_count // 2
    ).reshape(waves.shape + (lon_count // 2,))

    lane = jnp.arange(LANES, dtype=jnp.int32)
    lane_index = jnp.broadcast_to(jnp.where(south == 1, LANES - 1 - lane, lane), (8, LANES))
    packed = fourier(south[None], circles, circle, lane_index, dev_count)
    me = me_lev[None].astype(jnp.int32)
    pairs = lax.dynamic_slice_in_dim(pair_table, (me_lev * lat_count + me_lat) * slots, slots)
    rates = jnp.roll(damping_rates.reshape(levs, 1, group), -me_lev, axis=0)
    rates = jnp.broadcast_to(rates, (levs, 2, group)).reshape(-1, 1)
    packed, pairs, rates, me = lax.optimization_barrier((packed, pairs, rates, me))
    received = lax.all_to_all(
        packed, ("lev", "lat"), 0, 0, axis_index_groups=everyone, tiled=True
    ).reshape((lat_count, levs) + packed.shape[1:])

    basis = jnp.transpose(basis_table, (1, 2, 0))
    parts = []
    for first, count in CHUNKS:
        outs = legendre(
            first, count, me, pairs, received, basis, rates, lon_count, float(top * (top + 1))
        )
        moved = [outs[0]]
        for s in range(1, levs):
            to = [(i, (i + s) % levs) for i in range(levs)]
            moved.append(lax.ppermute(outs[s], "lev", to))
        parts.append(moved)
    return assemble(me, parts).reshape(slots, levs, 2, group, cols)


CHUNKS = ((0, 2), (2, 3))


def solution(mesh):
    placed = (P(None, "lat", "lev"), P(None, ("lev", "lat"), None), P(), P())
    return jax.shard_map(
        transform,
        mesh=mesh,
        in_specs=placed,
        out_specs=P("lat", None, None, "lev", None),
        check_vma=False,
    )
```

```python
import functools
import math

import jax
import jax.numpy as jnp
from jax import lax
from jax.experimental import pallas as pl
from jax.experimental.pallas import tpu as pltpu
from jax.sharding import PartitionSpec as P


F32 = jnp.float32
BF16 = jnp.bfloat16
NT = (((1,), (1,)), ((), ()))
LANES = 128


COS_TERMS = [((-1) ** n) * (2 * math.pi) ** (2 * n) / math.factorial(2 * n) for n in range(10)]


def cos_turns(turns):
    part = turns - jnp.floor(turns + 0.5)
    square = part * part
    total = jnp.full_like(square, COS_TERMS[-1])
    for term in COS_TERMS[-2::-1]:
        total = total * square + term
    return total


def circle_kernel(lon_count, wave_ref, quarter_ref, out_ref):
    rows, cols = out_ref.shape
    size = 64
    lane = lax.broadcasted_iota(jnp.int32, (size, LANES), 1).astype(F32)

    def block(i, carry):
        span = pl.ds(pl.multiple_of(i * size, size), size)
        wave = wave_ref[span, :].astype(F32)
        quarter = quarter_ref[span, :].astype(F32) * 0.25

        def turns(product):
            product = product - jnp.floor(product * (1.0 / lon_count)) * lon_count
            return product * (1.0 / lon_count)

        twice = 2.0 * cos_turns(turns(wave * float(LANES)))
        before = cos_turns(turns(wave * lane) + quarter)
        now = cos_turns(turns(wave * (lane + float(LANES))) + quarter)
        out_ref[span, :LANES] = before.astype(BF16)
        out_ref[span, LANES : 2 * LANES] = now.astype(BF16)
        for tile in range(2, cols // LANES):
            before, now = now, twice * now - before
            out_ref[span, tile * LANES : (tile + 1) * LANES] = now.astype(BF16)
        return carry

    lax.fori_loop(0, rows // size, block, 0)


def circle_table(waves, quarters, lon_count, cols):
    rows = waves.shape[0]
    return pl.pallas_call(
        functools.partial(circle_kernel, lon_count),
        in_specs=[VMEM_SPEC] * 2,
        out_specs=VMEM_SPEC,
        out_shape=jax.ShapeDtypeStruct((rows, cols), BF16),
        compiler_params=pltpu.CompilerParams(vmem_limit_bytes=CIRCLE_VMEM),
        cost_estimate=pl.CostEstimate(
            flops=rows * cols * 10, bytes_accessed=rows * cols * 2, transcendentals=0
        ),
        name="circle",
    )(waves, quarters)


VMEM_SPEC = pl.BlockSpec(memory_space=pltpu.VMEM)
HBM_SPEC = pl.BlockSpec(memory_space=pltpu.HBM)


def in_hbm(x):
    return pltpu.with_memory_space_constraint(x, pltpu.HBM)


CIRCLE_VMEM = 12 * 1024 * 1024


def fourier_kernel(
    south_ref, g_ref, table_ref, lane_ref, out_ref, circle_ref, fold_ref, tail_ref, sem
):
    _, bands, lats, quarter = g_ref.shape
    steps = circle_ref.shape[0]
    tiles = bands * lats // LANES
    end = out_ref.shape[1] - tiles * 16
    dests = out_ref.shape[0] // steps
    main = dests * 8
    south = south_ref[0]

    def table_copy(i):
        return pltpu.make_async_copy(table_ref.at[i], circle_ref.at[i], sem.at[i])

    for i in range(steps):
        table_copy(i).start()
    tail_ref[...] = jnp.zeros_like(tail_ref)

    def fold(j, carry):
        def squared(q):
            value = g_ref[q, pl.ds(2 * j, 2)].astype(F32)
            return (value * jnp.abs(value)).reshape(2 * lats, quarter)

        rows = pl.ds(pl.multiple_of(j * 2 * lats, 16), 2 * lats)
        for half in range(2):
            near, far = squared(half), squared(half + 2)
            cols = slice(half * quarter, (half + 1) * quarter)
            fold_ref[0, rows, cols] = (near + far).astype(BF16)
            fold_ref[1, rows, cols] = (near - far).astype(BF16)
        return carry

    lax.fori_loop(0, bands // 2, fold, 0)
    index = jnp.broadcast_to(lane_ref[0:1, :], (circle_ref.shape[2], LANES))

    def step(i, carry):
        table_copy(i).wait()
        span = pl.ds(i * dests, dests)
        for low in range(0, tiles, 2):
            many = min(2, tiles - low)
            rows = slice(low * LANES, (low + many) * LANES)
            values = [
                lax.dot_general(
                    circle_ref[i, kind], fold_ref[kind, rows, :], NT, preferred_element_type=F32
                )
                for kind in range(2)
            ]
            for at in range(many):
                place = jnp.where(south == 1, tiles - 1 - (low + at), low + at)
                both = []
                for kind in range(2):
                    value = jnp.take_along_axis(
                        values[kind][:, at * LANES : (at + 1) * LANES],
                        index,
                        axis=1,
                        mode="promise_in_bounds",
                    )
                    both.append(value[:main].reshape(dests, 8, LANES))
                    for r in range(2):
                        spot = pl.ds(place * 4 + kind * 2 + r, dests, stride=end)
                        tail_ref[spot, :] = value[main + r * dests : main + (r + 1) * dests]
                rows16 = pl.ds(pl.multiple_of(place * 16, 16), 16)
                out_ref[span, rows16, :] = jnp.concatenate(both, axis=1).astype(BF16)
        last = tail_ref[...].reshape(dests, end, LANES)
        out_ref[span, tiles * 16 :, :] = last.astype(BF16)
        return carry

    lax.fori_loop(0, steps, step, 0)


def fourier(south, received, circle, lane_index, dev_count):
    steps = circle.shape[0]
    dests = dev_count // steps
    _, bands, lats, quarter = received.shape
    lat_half = bands * lats
    tiles = lat_half // LANES
    end = -(-tiles * 4 // 8) * 8
    rows = tiles * 16 + end
    return pl.pallas_call(
        fourier_kernel,
        in_specs=[pl.BlockSpec(memory_space=pltpu.SMEM), VMEM_SPEC, HBM_SPEC, VMEM_SPEC],
        out_specs=VMEM_SPEC,
        scratch_shapes=[
            pltpu.VMEM(circle.shape, BF16),
            pltpu.VMEM((2, lat_half, 2 * quarter), BF16),
            pltpu.VMEM((dests * end, LANES), F32),
            pltpu.SemaphoreType.DMA((steps,)),
        ],
        out_shape=jax.ShapeDtypeStruct((dev_count, rows, LANES), BF16),
        compiler_params=pltpu.CompilerParams(vmem_limit_bytes=FOURIER_VMEM),
        cost_estimate=pl.CostEstimate(
            flops=2 * circle.size * lat_half,
            bytes_accessed=2 * (received.size + circle.size + dev_count * rows * LANES),
            transcendentals=0,
        ),
        name="fourier",
    )(south, received, in_hbm(circle), lane_index)


FOURIER_VMEM = 24 * 1024 * 1024
LEGENDRE_VMEM = 24 * 1024 * 1024


def gather_kernel(first, me_ref, recv_ref, basis_ref, x_ref, part_ref, main_ref, tail_ref, sem):
    levs = recv_ref.shape[1]
    group = recv_ref.shape[0] // 2
    slots, _, _, tiles, rows, _ = x_ref.shape
    end = recv_ref.shape[2] - tiles * 16
    part = rows // levs
    copies = slot_copies(basis_ref, part_ref, sem, first)
    for copy in copies:
        copy.start()

    def step(x, carry):
        base = lax.rem(x - me_ref[0] + levs, levs) * part

        def sides(span, height, into):
            n = recv_ref[:group, x, span, :].astype(F32).reshape(group * height, LANES)
            s = recv_ref[group:, x, span, :].astype(F32).reshape(group * height, LANES)
            into[0] = n + s
            into[1] = n - s

        def put(slot, kind, tile, r, from_ref, start, stride):
            dest = pl.ds(pl.multiple_of(base + r * group, 16), group)
            for par in range(2):
                value = from_ref[par, pl.ds(start, group, stride=stride), :]
                x_ref[slot, par, kind, tile, dest, :] = value.astype(BF16)

        for tile in range(tiles):
            sides(slice(tile * 16, tile * 16 + 16), 16, main_ref.at[tile])
            for kind in range(2):
                for k in range(slots - 1):
                    for r in range(2):
                        put(k, kind, tile, r, main_ref.at[tile], kind * 8 + k * 2 + r, 16)
        sides(slice(tiles * 16, tiles * 16 + end), end, tail_ref)
        for tile in range(tiles):
            for kind in range(2):
                for r in range(2):
                    put(slots - 1, kind, tile, r, tail_ref, tile * 4 + kind * 2 + r, end)
        return carry

    lax.fori_loop(0, levs, step, 0)
    for copy in copies:
        copy.wait()


def slot_copies(basis_ref, part_ref, sem, first):
    return [
        pltpu.make_async_copy(basis_ref.at[first + k], part_ref.at[k], sem.at[k])
        for k in range(part_ref.shape[0])
    ]


def gather(me, received, basis, chunk):
    slots, cols, lats = basis.shape
    lat_count, levs, rows, _ = received.shape
    group = lat_count // 2
    tiles = lats // LANES
    end = rows - tiles * 16
    first, count = chunk
    return pl.pallas_call(
        functools.partial(gather_kernel, first),
        in_specs=[pl.BlockSpec(memory_space=pltpu.SMEM), VMEM_SPEC, HBM_SPEC],
        out_specs=[VMEM_SPEC] * 2,
        scratch_shapes=[
            pltpu.VMEM((tiles, 2, group * 16, LANES), F32),
            pltpu.VMEM((2, group * end, LANES), F32),
            pltpu.SemaphoreType.DMA((count,)),
        ],
        out_shape=[
            jax.ShapeDtypeStruct((slots, 2, 2, tiles, levs * 2 * group, LANES), BF16),
            jax.ShapeDtypeStruct((count, cols, lats), BF16),
        ],
        compiler_params=pltpu.CompilerParams(vmem_limit_bytes=LEGENDRE_VMEM),
        cost_estimate=pl.CostEstimate(
            flops=20 * received.size, bytes_accessed=4 * received.size, transcendentals=0
        ),
        name="gather",
    )(me, received, in_hbm(basis))


def legendre_kernel(scale, norm, levs, first, ahead, pairs_ref, x_ref, basis_ref, rate_ref, *refs):
    copies = []
    if ahead is not None:
        all_ref, part_ref, sem = refs[0], refs[1 + levs], refs[2 + levs]
        copies = slot_copies(all_ref, part_ref, sem, ahead)
        refs = refs[1:]
    for copy in copies:
        copy.start()
    out_refs = refs[:levs]
    count = basis_ref.shape[0]
    waves = basis_ref.shape[1] - 1
    tiles, rows = x_ref.shape[3:5]
    part = rows // levs
    width = 256
    rates = jnp.concatenate([rate_ref[...]] * (width // LANES), axis=1)

    def slot_step(k, carry):
        pair = pairs_ref[k + first]
        bound = waves - pair
        first_kind = lax.rem(pair, 2)

        def damping(column, second):
            degree = jnp.where(second, column - 1, pair + column)
            scaled = (degree * (degree + 1)).astype(F32) / norm
            return scale / (1.0 + rates[:, : column.shape[1]] * (scaled * scaled))

        def emit(start, value):
            value = value.astype(BF16)
            for s in range(levs):
                out_refs[s][k, :, start : start + value.shape[1]] = value[s * part : (s + 1) * part]

        def side(par, kind):
            return jnp.concatenate([x_ref[k + first, par, kind, t] for t in range(tiles)], axis=1)

        def block(start):
            column = start + lax.broadcasted_iota(jnp.int32, (1, width), 1)
            second = column >= bound
            even = lax.rem(jnp.where(second, column + pair, column), 2) == 0
            factor = damping(column, second)
            basis = basis_ref[k, start : start + width, :]

            def product(kind):
                left = jnp.concatenate([side(0, kind), side(1, kind)], axis=0)
                both = lax.dot_general(left, basis, NT, preferred_element_type=F32)
                return jnp.where(even, both[:rows], both[rows:]) * factor

            value = product(jnp.where(start >= bound, 1 - first_kind, first_kind))
            emit(start, value)

            @pl.when((start < bound) & (bound < start + width))
            def _():
                emit(start, jnp.where(second, product(1 - first_kind), value))

        for start in range(0, waves, width):
            block(start)
        column = jnp.full((1, 1), waves, jnp.int32)
        left = side(first_kind, 1 - first_kind).astype(F32)
        final = jnp.sum(left * basis_ref[k, waves:, :].astype(F32), axis=1, keepdims=True)
        emit(waves, final * damping(column, column >= bound))
        return carry

    lax.fori_loop(0, count, slot_step, 0)
    for copy in copies:
        copy.wait()


def legendre(first, ahead, pairs, x, basis, basis_all, rates, levs, lon_count, norm):
    count, cols, lats = basis.shape
    part = x.shape[4] // levs
    specs = [pl.BlockSpec(memory_space=pltpu.SMEM), VMEM_SPEC, VMEM_SPEC, VMEM_SPEC]
    shapes = [jax.ShapeDtypeStruct((count, part, cols), BF16)] * levs
    operands, scratch = [pairs, x, basis, rates], []
    if ahead is not None:
        specs.append(HBM_SPEC)
        operands.append(in_hbm(basis_all))
        shapes.append(jax.ShapeDtypeStruct((ahead[1], cols, lats), BF16))
        scratch.append(pltpu.SemaphoreType.DMA((ahead[1],)))
    return pl.pallas_call(
        functools.partial(
            legendre_kernel, 1.0 / lon_count, norm, levs, first, ahead and ahead[0]
        ),
        in_specs=specs,
        out_specs=[VMEM_SPEC] * len(shapes),
        out_shape=shapes,
        scratch_shapes=scratch,
        compiler_params=pltpu.CompilerParams(vmem_limit_bytes=LEGENDRE_VMEM),
        cost_estimate=pl.CostEstimate(
            flops=2 * count * cols * lats * 256,
            bytes_accessed=2 * count * cols * (lats + 128),
            transcendentals=0,
        ),
        name="legendre",
    )(*operands)


def assemble_kernel(counts, me_ref, *refs):
    levs = refs[-2].shape[1]
    out_ref, sem = refs[-2:]
    copies, low = [], 0
    for c, count in enumerate(counts):
        for s in range(levs):
            lev = lax.rem(me_ref[0] - s + levs, levs)
            n = c * levs + s
            dest = out_ref.at[low : low + count, lev]
            copies.append(pltpu.make_async_copy(refs[n], dest, sem.at[n]))
        low += count
    for copy in copies:
        copy.start()
    for copy in copies:
        copy.wait()


def assemble(me, parts):
    levs = len(parts[0])
    _, part, cols = parts[0][0].shape
    counts = [p[0].shape[0] for p in parts]
    flat = [a for p in parts for a in p]
    anywhere = pl.BlockSpec(memory_space=pl.ANY)
    return pl.pallas_call(
        functools.partial(assemble_kernel, counts),
        in_specs=[pl.BlockSpec(memory_space=pltpu.SMEM)] + [anywhere] * len(flat),
        out_specs=anywhere,
        scratch_shapes=[pltpu.SemaphoreType.DMA((len(flat),))],
        out_shape=jax.ShapeDtypeStruct((sum(counts), levs, part, cols), BF16),
        compiler_params=pltpu.CompilerParams(vmem_limit_bytes=1024 * 1024),
        name="assemble",
    )(me, *flat)


def transform(grid_values, basis_table, damping_rates, pair_table):
    levs, lat_count = lax.axis_size("lev"), lax.axis_size("lat")
    dev_count = levs * lat_count
    half_bands = lat_count // 2
    lon_count = grid_values.shape[2] * levs
    slots, cols = basis_table.shape[1], basis_table.shape[2]
    top = cols - 2
    group = half_bands
    me_lev, me_lat = lax.axis_index("lev"), lax.axis_index("lat")
    south = (me_lat >= half_bands).astype(jnp.int32)

    halves = [
        [x * lat_count + h * half_bands + b for x in range(levs) for b in range(half_bands)]
        for h in range(2)
    ]
    everyone = [[x * lat_count + b for b in range(lat_count) for x in range(levs)]]
    circles = lax.all_to_all(
        grid_values, ("lev", "lat"), 0, 0, axis_index_groups=halves, tiled=True
    )
    circles = circles.reshape((levs, half_bands) + grid_values.shape[1:])

    steps = 2
    table = jnp.transpose(pair_table.reshape(levs, lat_count, slots), (1, 0, 2))
    table = table.reshape(steps, dev_count // steps, slots)
    other = top - table
    odd = table % 2 == 1
    kinds = []
    for wave in (jnp.where(odd, other, table), jnp.where(odd, table, other)):
        head = jnp.repeat(wave[:, :, : slots - 1], 2, axis=2).reshape(steps, -1)
        kinds.append(jnp.concatenate([head, wave[:, :, slots - 1], wave[:, :, slots - 1]], axis=1))
    waves = jnp.stack(kinds, axis=1)
    row = jnp.arange(waves.shape[2], dtype=jnp.int32)
    main = dev_count // steps * 2 * (slots - 1)
    quarters = jnp.where(row < main, row % 2, (row >= main + dev_count // steps).astype(jnp.int32))
    quarters = jnp.broadcast_to(quarters, waves.shape)
    lane = jnp.arange(LANES, dtype=jnp.int32)
    lane_index = jnp.broadcast_to(jnp.where(south == 1, LANES - 1 - lane, lane), (8, LANES))
    me = me_lev[None].astype(jnp.int32)
    pairs = lax.dynamic_slice_in_dim(pair_table, (me_lev * lat_count + me_lat) * slots, slots)
    rates = jnp.roll(damping_rates.reshape(levs, 1, group), -me_lev, axis=0)
    rates = jnp.broadcast_to(rates, (levs, 2, group)).reshape(-1, 1)
    rates = jnp.broadcast_to(rates, (rates.shape[0], LANES))
    spread = lambda v: jnp.broadcast_to(v.reshape(-1)[:, None], (v.size, LANES))
    wave_rows, quarter_rows, lane_index, south, me, pairs, rates = lax.optimization_barrier(
        (spread(waves), spread(quarters), lane_index, south[None], me, pairs, rates)
    )
    circle = circle_table(wave_rows, quarter_rows, lon_count, lon_count // 2)
    circle = circle.reshape(waves.shape + (lon_count // 2,))
    packed = fourier(south, circles, circle, lane_index, dev_count)
    received = lax.all_to_all(
        packed, ("lev", "lat"), 0, 0, axis_index_groups=everyone, tiled=True
    ).reshape((lat_count, levs) + packed.shape[1:])
    basis = jnp.transpose(basis_table, (1, 2, 0))
    x, ready = gather(me, received, basis, CHUNKS[0])
    parts = []
    for c, (first, count) in enumerate(CHUNKS):
        ahead = CHUNKS[c + 1] if c + 1 < len(CHUNKS) else None
        norm = float(top * (top + 1))
        outs = legendre(
            first, ahead, pairs, x, ready, basis, rates, levs, lon_count, norm
        )
        ready = outs[-1]
        moved = [outs[0]]
        for s in range(1, levs):
            to = [(i, (i + s) % levs) for i in range(levs)]
            moved.append(lax.ppermute(outs[s], "lev", to))
        parts.append(moved)
    return assemble(me, parts).reshape(slots, levs, 2, group, cols)


CHUNKS = ((0, 2), (2, 3))


def solution(mesh):
    placed = (P(None, "lat", "lev"), P(None, ("lev", "lat"), None), P(), P())
    return jax.shard_map(
        transform,
        mesh=mesh,
        in_specs=placed,
        out_specs=P("lat", None, None, "lev", None),
        check_vma=False,
    )
```

```python
import functools
import math

import jax
import jax.numpy as jnp
from jax import lax
from jax.experimental import pallas as pl
from jax.experimental.pallas import tpu as pltpu
from jax.sharding import PartitionSpec as P


F32 = jnp.float32
BF16 = jnp.bfloat16
NT = (((1,), (1,)), ((), ()))
NN = (((1,), (0,)), ((), ()))
LANES = 128


COS_TERMS = [((-1) ** n) * (2 * math.pi) ** (2 * n) / math.factorial(2 * n) for n in range(10)]


def cos_turns(turns):
    part = turns - jnp.floor(turns + 0.5)
    square = part * part
    total = jnp.full_like(square, COS_TERMS[-1])
    for term in COS_TERMS[-2::-1]:
        total = total * square + term
    return total


def circle_kernel(lon_count, wave_ref, quarter_ref, out_ref):
    rows, cols = out_ref.shape
    size = 64
    lane = lax.broadcasted_iota(jnp.int32, (size, LANES), 1).astype(F32)

    def block(i, carry):
        span = pl.ds(pl.multiple_of(i * size, size), size)
        wave = wave_ref[span, :].astype(F32)
        quarter = quarter_ref[span, :].astype(F32) * 0.25

        def turns(product):
            product = product - jnp.floor(product * (1.0 / lon_count)) * lon_count
            return product * (1.0 / lon_count)

        twice = 2.0 * cos_turns(turns(wave * float(LANES)))
        before = cos_turns(turns(wave * lane) + quarter)
        now = cos_turns(turns(wave * (lane + float(LANES))) + quarter)
        out_ref[span, :LANES] = before.astype(BF16)
        out_ref[span, LANES : 2 * LANES] = now.astype(BF16)
        for tile in range(2, cols // LANES):
            before, now = now, twice * now - before
            out_ref[span, tile * LANES : (tile + 1) * LANES] = now.astype(BF16)
        return carry

    lax.fori_loop(0, rows // size, block, 0)


def circle_table(waves, quarters, lon_count, cols):
    rows = waves.shape[0]
    return pl.pallas_call(
        functools.partial(circle_kernel, lon_count),
        in_specs=[VMEM_SPEC] * 2,
        out_specs=VMEM_SPEC,
        out_shape=jax.ShapeDtypeStruct((rows, cols), BF16),
        compiler_params=pltpu.CompilerParams(vmem_limit_bytes=CIRCLE_VMEM),
        cost_estimate=pl.CostEstimate(
            flops=rows * cols * 10, bytes_accessed=rows * cols * 2, transcendentals=0
        ),
        name="circle",
    )(waves, quarters)


VMEM_SPEC = pl.BlockSpec(memory_space=pltpu.VMEM)
HBM_SPEC = pl.BlockSpec(memory_space=pltpu.HBM)


def in_hbm(x):
    return pltpu.with_memory_space_constraint(x, pltpu.HBM)


CIRCLE_VMEM = 12 * 1024 * 1024


def fourier_kernel(
    south_ref, g_ref, table_ref, lane_ref, out_ref, circle_ref, fold_ref, tail_ref, sem
):
    _, cores, bands, lats, quarter = g_ref.shape
    bands = bands * cores
    steps = circle_ref.shape[0]
    tiles = bands * lats // LANES
    end = out_ref.shape[1] - tiles * 16
    dests = out_ref.shape[0] // steps
    main = dests * 8
    south = south_ref[0]

    def table_copy(i):
        return pltpu.make_async_copy(table_ref.at[i], circle_ref.at[i], sem.at[i])

    for i in range(steps):
        table_copy(i).start()
    tail_ref[...] = jnp.zeros_like(tail_ref)

    def fold(j, carry):
        def squared(q):
            value = g_ref[q, :, j].astype(F32)
            return (value * jnp.abs(value)).reshape(cores * lats, quarter)

        rows = pl.ds(pl.multiple_of(j * cores * lats, 16), cores * lats)
        for half in range(2):
            near, far = squared(half), squared(half + 2)
            cols = slice(half * quarter, (half + 1) * quarter)
            fold_ref[0, rows, cols] = (near + far).astype(BF16)
            fold_ref[1, rows, cols] = (near - far).astype(BF16)
        return carry

    lax.fori_loop(0, bands // cores, fold, 0)
    index = jnp.broadcast_to(lane_ref[0:1, :], (circle_ref.shape[2], LANES))

    def step(i, carry):
        table_copy(i).wait()
        span = pl.ds(i * dests, dests)
        for low in range(0, tiles, 2):
            many = min(2, tiles - low)
            rows = slice(low * LANES, (low + many) * LANES)
            values = [
                lax.dot_general(
                    circle_ref[i, kind], fold_ref[kind, rows, :], NT, preferred_element_type=F32
                )
                for kind in range(2)
            ]
            for at in range(many):
                place = jnp.where(south == 1, tiles - 1 - (low + at), low + at)
                both = []
                for kind in range(2):
                    value = jnp.take_along_axis(
                        values[kind][:, at * LANES : (at + 1) * LANES],
                        index,
                        axis=1,
                        mode="promise_in_bounds",
                    )
                    both.append(value[:main].reshape(dests, 8, LANES))
                    for r in range(2):
                        spot = pl.ds(place * 4 + kind * 2 + r, dests, stride=end)
                        tail_ref[spot, :] = value[main + r * dests : main + (r + 1) * dests]
                rows16 = pl.ds(pl.multiple_of(place * 16, 16), 16)
                out_ref[span, rows16, :] = jnp.concatenate(both, axis=1).astype(BF16)
        last = tail_ref[...].reshape(dests, end, LANES)
        out_ref[span, tiles * 16 :, :] = last.astype(BF16)
        return carry

    lax.fori_loop(0, steps, step, 0)


def fourier(south, received, circle, lane_index, dev_count):
    steps = circle.shape[0]
    dests = dev_count // steps
    _, cores, bands, lats, quarter = received.shape
    lat_half = cores * bands * lats
    tiles = lat_half // LANES
    end = -(-tiles * 4 // 8) * 8
    rows = tiles * 16 + end
    return pl.pallas_call(
        fourier_kernel,
        in_specs=[pl.BlockSpec(memory_space=pltpu.SMEM), VMEM_SPEC, HBM_SPEC, VMEM_SPEC],
        out_specs=VMEM_SPEC,
        scratch_shapes=[
            pltpu.VMEM(circle.shape, BF16),
            pltpu.VMEM((2, lat_half, 2 * quarter), BF16),
            pltpu.VMEM((dests * end, LANES), F32),
            pltpu.SemaphoreType.DMA((steps,)),
        ],
        out_shape=jax.ShapeDtypeStruct((dev_count, rows, LANES), BF16),
        compiler_params=pltpu.CompilerParams(vmem_limit_bytes=FOURIER_VMEM),
        cost_estimate=pl.CostEstimate(
            flops=2 * circle.size * lat_half,
            bytes_accessed=2 * (received.size + circle.size + dev_count * rows * LANES),
            transcendentals=0,
        ),
        name="fourier",
    )(south, received, in_hbm(circle), lane_index)


FOURIER_VMEM = 24 * 1024 * 1024
LEGENDRE_VMEM = 24 * 1024 * 1024


def gather_kernel(first, total, me_ref, recv_ref, x_ref, main_ref, tail_ref):
    levs, nc, ny, nz = recv_ref.shape[:4]
    group = nc * ny * nz // 2
    count, _, _, tiles, rows, _ = x_ref.shape
    mains = range(first, min(first + count, total - 1))
    end = recv_ref.shape[4] - tiles * 16
    part = rows // levs

    def step(x, carry):
        base = lax.rem(x - me_ref[0] + levs, levs) * part

        def sides(span, height, into):
            n = recv_ref[x, :, : ny // 2, :, span, :].astype(F32).reshape(group * height, LANES)
            s = recv_ref[x, :, ny // 2 :, :, span, :].astype(F32).reshape(group * height, LANES)
            into[0] = n + s
            into[1] = n - s

        def put(slot, kind, tile, r, from_ref, start, stride):
            dest = pl.ds(pl.multiple_of(base + r * group, 16), group)
            for par in range(2):
                value = from_ref[par, pl.ds(start, group, stride=stride), :]
                x_ref[slot - first, par, kind, tile, dest, :] = value.astype(BF16)

        for tile in range(tiles):
            sides(slice(tile * 16, tile * 16 + 16), 16, main_ref.at[tile])
            for kind in range(2):
                for k in mains:
                    for r in range(2):
                        put(k, kind, tile, r, main_ref.at[tile], kind * 8 + k * 2 + r, 16)
        if first + count == total:
            sides(slice(tiles * 16, tiles * 16 + end), end, tail_ref)
            for tile in range(tiles):
                for kind in range(2):
                    for r in range(2):
                        put(total - 1, kind, tile, r, tail_ref, tile * 4 + kind * 2 + r, end)
        return carry

    lax.fori_loop(0, levs, step, 0)


def turn_kernel(basis_ref, out_ref, last_ref):
    lats, waves = out_ref.shape[1:]
    size = 256
    row = lax.broadcasted_iota(jnp.int32, (size, size), 0)
    eye = (row == lax.broadcasted_iota(jnp.int32, (size, size), 1)).astype(BF16)
    for start in range(0, waves, size):
        for low in range(0, lats, size):
            high = min(low + size, lats)
            out_ref[0, low:high, start : start + size] = lax.dot_general(
                eye[: high - low, : high - low],
                basis_ref[0, start : start + size, low:high],
                NT,
                preferred_element_type=F32,
            ).astype(BF16)
    last_ref[0] = basis_ref[0, waves:, :]


def turn(basis):
    slots, cols, lats = basis.shape
    return pl.pallas_call(
        turn_kernel,
        grid=(slots,),
        in_specs=[pl.BlockSpec((1, cols, lats), lambda k: (k, 0, 0))],
        out_specs=[
            pl.BlockSpec((1, lats, cols - 1), lambda k: (k, 0, 0)),
            pl.BlockSpec((1, 1, lats), lambda k: (k, 0, 0)),
        ],
        out_shape=[
            jax.ShapeDtypeStruct((slots, lats, cols - 1), BF16),
            jax.ShapeDtypeStruct((slots, 1, lats), BF16),
        ],
        compiler_params=pltpu.CompilerParams(vmem_limit_bytes=LEGENDRE_VMEM),
        cost_estimate=pl.CostEstimate(
            flops=2 * 256 * basis.size, bytes_accessed=4 * basis.size, transcendentals=0
        ),
        name="turn",
    )(basis)


def gather(first, count, me, received, slots, lats):
    levs, nc, ny, nz, rows, _ = received.shape
    group = nc * ny * nz // 2
    tiles = lats // LANES
    end = rows - tiles * 16
    return pl.pallas_call(
        functools.partial(gather_kernel, first, slots),
        in_specs=[pl.BlockSpec(memory_space=pltpu.SMEM), VMEM_SPEC],
        out_specs=VMEM_SPEC,
        scratch_shapes=[
            pltpu.VMEM((tiles, 2, group * 16, LANES), F32),
            pltpu.VMEM((2, group * end, LANES), F32),
        ],
        out_shape=jax.ShapeDtypeStruct((count, 2, 2, tiles, levs * 2 * group, LANES), BF16),
        compiler_params=pltpu.CompilerParams(vmem_limit_bytes=LEGENDRE_VMEM),
        cost_estimate=pl.CostEstimate(
            flops=20 * received.size, bytes_accessed=4 * received.size, transcendentals=0
        ),
        name="gather",
    )(me, received)


def legendre_kernel(
    scale, norm, first, count, pairs_ref, x_ref, basis_ref, last_ref, rate_ref, *out_refs
):
    levs = len(out_refs)
    waves = basis_ref.shape[2]
    tiles, rows = x_ref.shape[3:5]
    part = rows // levs
    width = 256
    rates = jnp.concatenate([rate_ref[...]] * (width // LANES), axis=1)

    def slot_step(k):
        pair = pairs_ref[k + first]
        bound = waves - pair
        first_kind = lax.rem(pair, 2)

        def damping(column, second):
            degree = jnp.where(second, column - 1, pair + column)
            scaled = (degree * (degree + 1)).astype(F32) / norm
            return scale / (1.0 + rates[:, : column.shape[1]] * (scaled * scaled))

        def side(par, kind):
            return jnp.concatenate([x_ref[k, par, kind, t] for t in range(tiles)], axis=1)

        def product(start, kind):
            column = start + lax.broadcasted_iota(jnp.int32, (1, width), 1)
            second = column >= bound
            even = lax.rem(jnp.where(second, column + pair, column), 2) == 0
            left = jnp.concatenate([side(0, kind), side(1, kind)], axis=0)
            basis = basis_ref[k + first, :, pl.ds(start, width)]
            both = lax.dot_general(left, basis, NN, preferred_element_type=F32)
            value = jnp.where(even, both[:rows], both[rows:]) * damping(column, second)
            return value.astype(BF16), second

        for start in range(0, waves, width):
            value, _ = product(start, jnp.where(start >= bound, 1 - first_kind, first_kind))
            for s in range(levs):
                out_refs[s][k, :, start : start + width] = value[s * part : (s + 1) * part]
        start = pl.multiple_of(jnp.minimum(bound // width, waves // width - 1) * width, width)
        value, second = product(start, 1 - first_kind)
        for s in range(levs):
            spot = (k, slice(None), pl.ds(start, width))
            kept = jnp.where(second, value[s * part : (s + 1) * part].astype(F32), out_refs[s][spot].astype(F32))
            out_refs[s][spot] = kept.astype(BF16)
        column = jnp.full((1, 1), waves, jnp.int32)
        left = side(first_kind, 1 - first_kind).astype(F32)
        final = jnp.sum(left * last_ref[k + first].astype(F32), axis=1, keepdims=True)
        final = (final * damping(column, column >= bound)).astype(BF16)
        for s in range(levs):
            out_refs[s][k, :, waves:] = final[s * part : (s + 1) * part]

    for k in range(count):
        slot_step(k)


def legendre(first, count, pairs, x, basis, last, rates, levs, lon_count, norm):
    _, lats, waves = basis.shape
    cols = waves + 1
    part = x.shape[4] // levs
    return pl.pallas_call(
        functools.partial(legendre_kernel, 1.0 / lon_count, norm, first, count),
        in_specs=[pl.BlockSpec(memory_space=pltpu.SMEM)] + [VMEM_SPEC] * 4,
        out_specs=[VMEM_SPEC] * levs,
        out_shape=[jax.ShapeDtypeStruct((count, part, cols), BF16)] * levs,
        compiler_params=pltpu.CompilerParams(vmem_limit_bytes=LEGENDRE_VMEM),
        cost_estimate=pl.CostEstimate(
            flops=2 * count * cols * lats * 256,
            bytes_accessed=2 * count * cols * (lats + 128),
            transcendentals=0,
        ),
        name="legendre",
    )(pairs, x, basis, last, rates)


def assemble_kernel(counts, me_ref, *refs):
    levs = refs[-2].shape[1]
    out_ref, sem = refs[-2:]
    copies, low = [], 0
    for c, count in enumerate(counts):
        for s in range(levs):
            lev = lax.rem(me_ref[0] - s + levs, levs)
            n = c * levs + s
            dest = out_ref.at[low : low + count, lev]
            copies.append(pltpu.make_async_copy(refs[n], dest, sem.at[n]))
        low += count
    for copy in copies:
        copy.start()
    for copy in copies:
        copy.wait()


def assemble(me, parts):
    levs = len(parts[0])
    _, part, cols = parts[0][0].shape
    counts = [p[0].shape[0] for p in parts]
    flat = [a for p in parts for a in p]
    anywhere = pl.BlockSpec(memory_space=pl.ANY)
    return pl.pallas_call(
        functools.partial(assemble_kernel, counts),
        in_specs=[pl.BlockSpec(memory_space=pltpu.SMEM)] + [anywhere] * len(flat),
        out_specs=anywhere,
        scratch_shapes=[pltpu.SemaphoreType.DMA((len(flat),))],
        out_shape=jax.ShapeDtypeStruct((sum(counts), levs, part, cols), BF16),
        compiler_params=pltpu.CompilerParams(vmem_limit_bytes=1024 * 1024),
        name="assemble",
    )(me, *flat)


def transform(grid_values, basis_table, damping_rates, pair_table):
    levs, lat_count = lax.axis_size("lev"), lax.axis_size("lat")
    dev_count = levs * lat_count
    half_bands = lat_count // 2
    lon_count = grid_values.shape[2] * levs
    slots, cols = basis_table.shape[1], basis_table.shape[2]
    top = cols - 2
    lat_half = basis_table.shape[0]
    group = half_bands
    me_lev, me_lat = lax.axis_index("lev"), lax.axis_index("lat")
    south = (me_lat >= half_bands).astype(jnp.int32)

    ny, nz, nc = LAT_AXES
    at = lambda x, y, z, c: x * lat_count + (y * nz + z) * nc + c
    halves = [
        [
            at(x, y + h * ny // 2, z, c)
            for x in range(levs)
            for c in range(nc)
            for y in range(ny // 2)
            for z in range(nz)
        ]
        for h in range(2)
    ]
    everyone = [
        [at(x, y, z, c) for x in range(levs) for c in range(nc) for y in range(ny) for z in range(nz)]
    ]
    circles = lax.all_to_all(
        grid_values, ("lev", "lat"), 0, 0, axis_index_groups=halves, tiled=True
    )
    circles = circles.reshape((levs, nc, half_bands // nc) + grid_values.shape[1:])

    steps = 2
    table = jnp.transpose(pair_table.reshape(levs, ny, nz, nc, slots), (0, 3, 1, 2, 4))
    table = table.reshape(steps, dev_count // steps, slots)
    other = top - table
    odd = table % 2 == 1
    kinds = []
    for wave in (jnp.where(odd, other, table), jnp.where(odd, table, other)):
        head = jnp.repeat(wave[:, :, : slots - 1], 2, axis=2).reshape(steps, -1)
        kinds.append(jnp.concatenate([head, wave[:, :, slots - 1], wave[:, :, slots - 1]], axis=1))
    waves = jnp.stack(kinds, axis=1)
    row = jnp.arange(waves.shape[2], dtype=jnp.int32)
    main = dev_count // steps * 2 * (slots - 1)
    quarters = jnp.where(row < main, row % 2, (row >= main + dev_count // steps).astype(jnp.int32))
    quarters = jnp.broadcast_to(quarters, waves.shape)
    lane = jnp.arange(LANES, dtype=jnp.int32)
    lane_index = jnp.broadcast_to(jnp.where(south == 1, LANES - 1 - lane, lane), (8, LANES))
    me = me_lev[None].astype(jnp.int32)
    pairs = lax.dynamic_slice_in_dim(pair_table, (me_lev * lat_count + me_lat) * slots, slots)
    rates = jnp.roll(damping_rates.reshape(levs, 1, group), -me_lev, axis=0)
    rates = jnp.broadcast_to(rates, (levs, 2, group)).reshape(-1, 1)
    rates = jnp.broadcast_to(rates, (rates.shape[0], LANES))
    spread = lambda v: jnp.broadcast_to(v.reshape(-1)[:, None], (v.size, LANES))
    wave_rows, quarter_rows, lane_index, south, me, pairs, rates = lax.optimization_barrier(
        (spread(waves), spread(quarters), lane_index, south[None], me, pairs, rates)
    )
    basis, last = turn(jnp.transpose(basis_table, (1, 2, 0)))
    circle = circle_table(wave_rows, quarter_rows, lon_count, lon_count // 2)
    circle = circle.reshape(waves.shape + (lon_count // 2,))
    packed = fourier(south, circles, circle, lane_index, dev_count)
    received = lax.all_to_all(
        packed, ("lev", "lat"), 0, 0, axis_index_groups=everyone, tiled=True
    ).reshape((levs, nc, ny, nz) + packed.shape[1:])
    parts = []
    for first, count in CHUNKS:
        norm = float(top * (top + 1))
        x = gather(first, count, me, received, slots, lat_half)
        outs = legendre(first, count, pairs, x, basis, last, rates, levs, lon_count, norm)
        moved = [outs[0]]
        for s in range(1, levs):
            to = [(i, (i + s) % levs) for i in range(levs)]
            moved.append(lax.ppermute(outs[s], "lev", to))
        parts.append(moved)
    return assemble(me, parts).reshape(slots, levs, 2, group, cols)


CHUNKS = ((0, 2), (2, 3))
LAT_AXES = (4, 4, 2)


def solution(mesh):
    placed = (P(None, "lat", "lev"), P(None, ("lev", "lat"), None), P(), P())
    return jax.shard_map(
        transform,
        mesh=mesh,
        in_specs=placed,
        out_specs=P("lat", None, None, "lev", None),
        check_vma=False,
    )
```

```python
import functools
import math

import jax
import jax.numpy as jnp
from jax import lax
from jax.experimental import pallas as pl
from jax.experimental.pallas import tpu as pltpu
from jax.sharding import PartitionSpec as P


F32 = jnp.float32
BF16 = jnp.bfloat16
NT = (((1,), (1,)), ((), ()))
NN = (((1,), (0,)), ((), ()))
LANES = 128


COS_TERMS = [((-1) ** n) * (2 * math.pi) ** (2 * n) / math.factorial(2 * n) for n in range(10)]


def cos_turns(turns):
    part = turns - jnp.floor(turns + 0.5)
    square = part * part
    total = jnp.full_like(square, COS_TERMS[-1])
    for term in COS_TERMS[-2::-1]:
        total = total * square + term
    return total


def circle_kernel(lon_count, wave_ref, quarter_ref, out_ref):
    rows, cols = out_ref.shape
    size = 64
    lane = lax.broadcasted_iota(jnp.int32, (size, LANES), 1).astype(F32)

    def block(i, carry):
        span = pl.ds(pl.multiple_of(i * size, size), size)
        wave = wave_ref[span, :].astype(F32)
        quarter = quarter_ref[span, :].astype(F32) * 0.25

        def turns(product):
            product = product - jnp.floor(product * (1.0 / lon_count)) * lon_count
            return product * (1.0 / lon_count)

        twice = 2.0 * cos_turns(turns(wave * float(LANES)))
        before = cos_turns(turns(wave * lane) + quarter)
        now = cos_turns(turns(wave * (lane + float(LANES))) + quarter)
        out_ref[span, :LANES] = before.astype(BF16)
        out_ref[span, LANES : 2 * LANES] = now.astype(BF16)
        for tile in range(2, cols // LANES):
            before, now = now, twice * now - before
            out_ref[span, tile * LANES : (tile + 1) * LANES] = now.astype(BF16)
        return carry

    lax.fori_loop(0, rows // size, block, 0)


def circle_table(waves, quarters, lon_count, cols):
    rows = waves.shape[0]
    return pl.pallas_call(
        functools.partial(circle_kernel, lon_count),
        in_specs=[VMEM_SPEC] * 2,
        out_specs=VMEM_SPEC,
        out_shape=jax.ShapeDtypeStruct((rows, cols), BF16),
        compiler_params=pltpu.CompilerParams(vmem_limit_bytes=CIRCLE_VMEM),
        cost_estimate=pl.CostEstimate(
            flops=rows * cols * 10, bytes_accessed=rows * cols * 2, transcendentals=0
        ),
        name="circle",
    )(waves, quarters)


VMEM_SPEC = pl.BlockSpec(memory_space=pltpu.VMEM)
HBM_SPEC = pl.BlockSpec(memory_space=pltpu.HBM)


def in_hbm(x):
    return pltpu.with_memory_space_constraint(x, pltpu.HBM)


CIRCLE_VMEM = 12 * 1024 * 1024


def fourier_kernel(
    south_ref, g_ref, table_ref, lane_ref, out_ref, circle_ref, fold_ref, tail_ref, sem
):
    _, cores, bands, lats, quarter = g_ref.shape
    bands = bands * cores
    steps = circle_ref.shape[0]
    tiles = bands * lats // LANES
    end = out_ref.shape[1] - tiles * 16
    dests = out_ref.shape[0] // steps
    main = dests * 8
    south = south_ref[0]

    def table_copy(i):
        return pltpu.make_async_copy(table_ref.at[i], circle_ref.at[i], sem.at[i])

    for i in range(steps):
        table_copy(i).start()
    tail_ref[...] = jnp.zeros_like(tail_ref)

    def fold(j, carry):
        def squared(q):
            value = g_ref[q, :, j].astype(F32)
            return (value * jnp.abs(value)).reshape(cores * lats, quarter)

        rows = pl.ds(pl.multiple_of(j * cores * lats, 16), cores * lats)
        for half in range(2):
            near, far = squared(half), squared(half + 2)
            cols = slice(half * quarter, (half + 1) * quarter)
            fold_ref[0, rows, cols] = (near + far).astype(BF16)
            fold_ref[1, rows, cols] = (near - far).astype(BF16)
        return carry

    lax.fori_loop(0, bands // cores, fold, 0)
    index = jnp.broadcast_to(lane_ref[0:1, :], (circle_ref.shape[2], LANES))

    def step(i, carry):
        table_copy(i).wait()
        span = pl.ds(i * dests, dests)
        for low in range(0, tiles, 2):
            many = min(2, tiles - low)
            rows = slice(low * LANES, (low + many) * LANES)
            values = [
                lax.dot_general(
                    circle_ref[i, kind], fold_ref[kind, rows, :], NT, preferred_element_type=F32
                )
                for kind in range(2)
            ]
            for at in range(many):
                place = jnp.where(south == 1, tiles - 1 - (low + at), low + at)
                both = []
                for kind in range(2):
                    value = jnp.take_along_axis(
                        values[kind][:, at * LANES : (at + 1) * LANES],
                        index,
                        axis=1,
                        mode="promise_in_bounds",
                    )
                    both.append(value[:main].reshape(dests, 8, LANES))
                    for r in range(2):
                        spot = pl.ds(place * 4 + kind * 2 + r, dests, stride=end)
                        tail_ref[spot, :] = value[main + r * dests : main + (r + 1) * dests]
                rows16 = pl.ds(pl.multiple_of(place * 16, 16), 16)
                out_ref[span, rows16, :] = jnp.concatenate(both, axis=1).astype(BF16)
        last = tail_ref[...].reshape(dests, end, LANES)
        out_ref[span, tiles * 16 :, :] = last.astype(BF16)
        return carry

    lax.fori_loop(0, steps, step, 0)


def fourier(south, received, circle, lane_index, dev_count):
    steps = circle.shape[0]
    dests = dev_count // steps
    _, cores, bands, lats, quarter = received.shape
    lat_half = cores * bands * lats
    tiles = lat_half // LANES
    end = -(-tiles * 4 // 8) * 8
    rows = tiles * 16 + end
    return pl.pallas_call(
        fourier_kernel,
        in_specs=[pl.BlockSpec(memory_space=pltpu.SMEM), VMEM_SPEC, HBM_SPEC, VMEM_SPEC],
        out_specs=VMEM_SPEC,
        scratch_shapes=[
            pltpu.VMEM(circle.shape, BF16),
            pltpu.VMEM((2, lat_half, 2 * quarter), BF16),
            pltpu.VMEM((dests * end, LANES), F32),
            pltpu.SemaphoreType.DMA((steps,)),
        ],
        out_shape=jax.ShapeDtypeStruct((dev_count, rows, LANES), BF16),
        compiler_params=pltpu.CompilerParams(vmem_limit_bytes=FOURIER_VMEM),
        cost_estimate=pl.CostEstimate(
            flops=2 * circle.size * lat_half,
            bytes_accessed=2 * (received.size + circle.size + dev_count * rows * LANES),
            transcendentals=0,
        ),
        name="fourier",
    )(south, received, in_hbm(circle), lane_index)


FOURIER_VMEM = 24 * 1024 * 1024
LEGENDRE_VMEM = 24 * 1024 * 1024


def gather_kernel(first, total, me_ref, recv_ref, x_ref, main_ref, tail_ref):
    levs, nc, ny, nz = recv_ref.shape[:4]
    group = nc * ny * nz // 2
    count, _, _, tiles, rows, _ = x_ref.shape
    mains = range(first, min(first + count, total - 1))
    end = recv_ref.shape[4] - tiles * 16
    part = rows // levs

    def step(x, carry):
        base = lax.rem(x - me_ref[0] + levs, levs) * part

        def sides(span, height, into):
            n = recv_ref[x, :, : ny // 2, :, span, :].astype(F32).reshape(group * height, LANES)
            s = recv_ref[x, :, ny // 2 :, :, span, :].astype(F32).reshape(group * height, LANES)
            into[0] = n + s
            into[1] = n - s

        def put(slot, kind, tile, r, from_ref, start, stride):
            dest = pl.ds(pl.multiple_of(base + r * group, 16), group)
            for par in range(2):
                value = from_ref[par, pl.ds(start, group, stride=stride), :]
                x_ref[slot - first, par, kind, tile, dest, :] = value.astype(BF16)

        for tile in range(tiles):
            sides(slice(tile * 16, tile * 16 + 16), 16, main_ref.at[tile])
            for kind in range(2):
                for k in mains:
                    for r in range(2):
                        put(k, kind, tile, r, main_ref.at[tile], kind * 8 + k * 2 + r, 16)
        if first + count == total:
            sides(slice(tiles * 16, tiles * 16 + end), end, tail_ref)
            for tile in range(tiles):
                for kind in range(2):
                    for r in range(2):
                        put(total - 1, kind, tile, r, tail_ref, tile * 4 + kind * 2 + r, end)
        return carry

    lax.fori_loop(0, levs, step, 0)


def turn_kernel(basis_ref, out_ref, last_ref):
    lats, waves = out_ref.shape[1:]
    size = 256
    row = lax.broadcasted_iota(jnp.int32, (size, size), 0)
    eye = (row == lax.broadcasted_iota(jnp.int32, (size, size), 1)).astype(BF16)
    for start in range(0, waves, size):
        for low in range(0, lats, size):
            high = min(low + size, lats)
            out_ref[0, low:high, start : start + size] = lax.dot_general(
                eye[: high - low, : high - low],
                basis_ref[0, start : start + size, low:high],
                NT,
                preferred_element_type=F32,
            ).astype(BF16)
    last_ref[0] = basis_ref[0, waves:, :]


def turn(basis):
    slots, cols, lats = basis.shape
    return pl.pallas_call(
        turn_kernel,
        grid=(slots,),
        in_specs=[pl.BlockSpec((1, cols, lats), lambda k: (k, 0, 0))],
        out_specs=[
            pl.BlockSpec((1, lats, cols - 1), lambda k: (k, 0, 0)),
            pl.BlockSpec((1, 1, lats), lambda k: (k, 0, 0)),
        ],
        out_shape=[
            jax.ShapeDtypeStruct((slots, lats, cols - 1), BF16),
            jax.ShapeDtypeStruct((slots, 1, lats), BF16),
        ],
        compiler_params=pltpu.CompilerParams(vmem_limit_bytes=LEGENDRE_VMEM),
        cost_estimate=pl.CostEstimate(
            flops=2 * 256 * basis.size, bytes_accessed=4 * basis.size, transcendentals=0
        ),
        name="turn",
    )(basis)


def gather(first, count, me, received, slots, lats):
    levs, nc, ny, nz, rows, _ = received.shape
    group = nc * ny * nz // 2
    tiles = lats // LANES
    end = rows - tiles * 16
    return pl.pallas_call(
        functools.partial(gather_kernel, first, slots),
        in_specs=[pl.BlockSpec(memory_space=pltpu.SMEM), VMEM_SPEC],
        out_specs=VMEM_SPEC,
        scratch_shapes=[
            pltpu.VMEM((tiles, 2, group * 16, LANES), F32),
            pltpu.VMEM((2, group * end, LANES), F32),
        ],
        out_shape=jax.ShapeDtypeStruct((count, 2, 2, tiles, levs * 2 * group, LANES), BF16),
        compiler_params=pltpu.CompilerParams(vmem_limit_bytes=LEGENDRE_VMEM),
        cost_estimate=pl.CostEstimate(
            flops=20 * received.size, bytes_accessed=4 * received.size, transcendentals=0
        ),
        name="gather",
    )(me, received)


def legendre_kernel(
    scale, norm, levs, first, count, pairs_ref, x_ref, basis_ref, last_ref, rate_ref, *refs
):
    out_refs, edge_refs = refs[-2 * levs : -levs], refs[-levs:]
    before = refs[: -2 * levs]
    waves = basis_ref.shape[2]
    tiles, rows = x_ref.shape[3:5]
    part = rows // levs
    width = 256
    rates = jnp.concatenate([rate_ref[...]] * (width // LANES), axis=1)

    def slot_step(k):
        pair = pairs_ref[k + first]
        bound = waves - pair
        first_kind = lax.rem(pair, 2)

        def damping(column, second):
            degree = jnp.where(second, column - 1, pair + column)
            scaled = (degree * (degree + 1)).astype(F32) / norm
            return scale / (1.0 + rates[:, : column.shape[1]] * (scaled * scaled))

        def side(par, kind):
            return jnp.concatenate([x_ref[k, par, kind, t] for t in range(tiles)], axis=1)

        def product(start, kind):
            column = start + lax.broadcasted_iota(jnp.int32, (1, width), 1)
            second = column >= bound
            even = lax.rem(jnp.where(second, column + pair, column), 2) == 0
            left = jnp.concatenate([side(0, kind), side(1, kind)], axis=0)
            basis = basis_ref[k + first, :, pl.ds(start, width)]
            both = lax.dot_general(left, basis, NN, preferred_element_type=F32)
            value = jnp.where(even, both[:rows], both[rows:]) * damping(column, second)
            return value.astype(BF16), second

        for start in range(0, waves, width):
            value, _ = product(start, jnp.where(start >= bound, 1 - first_kind, first_kind))
            for s in range(levs):
                out_refs[s][k, :, start : start + width] = value[s * part : (s + 1) * part]
        start = pl.multiple_of(jnp.minimum(bound // width, waves // width - 1) * width, width)
        value, second = product(start, 1 - first_kind)
        for s in range(levs):
            spot = (k, slice(None), pl.ds(start, width))
            kept = jnp.where(second, value[s * part : (s + 1) * part].astype(F32), out_refs[s][spot].astype(F32))
            out_refs[s][spot] = kept.astype(BF16)
        column = jnp.full((1, 1), waves, jnp.int32)
        left = side(first_kind, 1 - first_kind).astype(F32)
        final = jnp.sum(left * last_ref[k + first].astype(F32), axis=1, keepdims=True)
        return final * damping(column, column >= bound)

    lane = lax.broadcasted_iota(jnp.int32, (rows, LANES), 1)
    edge = jnp.zeros((rows, LANES), F32)
    if before:
        edge = jnp.concatenate([b[...].astype(F32) for b in before], axis=0)
    for k in range(count):
        edge = jnp.where(lane == k + first, slot_step(k), edge)
    for s in range(levs):
        edge_refs[s][...] = edge[s * part : (s + 1) * part].astype(BF16)


def legendre(first, count, pairs, x, basis, last, rates, before, levs, lon_count, norm):
    _, lats, waves = basis.shape
    cols = waves
    part = x.shape[4] // levs
    return pl.pallas_call(
        functools.partial(legendre_kernel, 1.0 / lon_count, norm, levs, first, count),
        in_specs=[pl.BlockSpec(memory_space=pltpu.SMEM)] + [VMEM_SPEC] * (4 + len(before)),
        out_specs=[VMEM_SPEC] * (2 * levs),
        out_shape=[jax.ShapeDtypeStruct((count, part, cols), BF16)] * levs
        + [jax.ShapeDtypeStruct((part, LANES), BF16)] * levs,
        compiler_params=pltpu.CompilerParams(vmem_limit_bytes=LEGENDRE_VMEM),
        cost_estimate=pl.CostEstimate(
            flops=2 * count * cols * lats * 256,
            bytes_accessed=2 * count * cols * (lats + 128),
            transcendentals=0,
        ),
        name="legendre",
    )(pairs, x, basis, last, rates, *before)


def assemble_kernel(counts, me_ref, *refs):
    out_ref = refs[-1]
    slots, levs, _, cols = out_ref.shape
    for s in range(levs):
        lev = lax.rem(me_ref[0] - s + levs, levs)
        low = 0
        for c, count in enumerate(counts):
            for k in range(count):
                out_ref[low + k, lev, :, : cols - 1] = refs[c * levs + s][k]
            low += count
        edge = refs[len(counts) * levs + s][...]
        for k in range(slots):
            out_ref[k, lev, :, cols - 1 :] = edge[:, k : k + 1]


def assemble(me, parts, edges):
    levs = len(edges)
    _, part, waves = parts[0][0].shape
    counts = [p[0].shape[0] for p in parts]
    flat = [a for p in parts for a in p] + edges
    return pl.pallas_call(
        functools.partial(assemble_kernel, counts),
        in_specs=[pl.BlockSpec(memory_space=pltpu.SMEM)] + [VMEM_SPEC] * len(flat),
        out_specs=VMEM_SPEC,
        out_shape=jax.ShapeDtypeStruct((sum(counts), levs, part, waves + 1), BF16),
        compiler_params=pltpu.CompilerParams(vmem_limit_bytes=LEGENDRE_VMEM),
        name="assemble",
    )(me, *flat)


def transform(grid_values, basis_table, damping_rates, pair_table):
    levs, lat_count = lax.axis_size("lev"), lax.axis_size("lat")
    dev_count = levs * lat_count
    half_bands = lat_count // 2
    lon_count = grid_values.shape[2] * levs
    slots, cols = basis_table.shape[1], basis_table.shape[2]
    top = cols - 2
    lat_half = basis_table.shape[0]
    group = half_bands
    me_lev, me_lat = lax.axis_index("lev"), lax.axis_index("lat")
    south = (me_lat >= half_bands).astype(jnp.int32)

    ny, nz, nc = LAT_AXES
    at = lambda x, y, z, c: x * lat_count + (y * nz + z) * nc + c
    halves = [
        [
            at(x, y + h * ny // 2, z, c)
            for x in range(levs)
            for c in range(nc)
            for y in range(ny // 2)
            for z in range(nz)
        ]
        for h in range(2)
    ]
    everyone = [
        [at(x, y, z, c) for x in range(levs) for c in range(nc) for y in range(ny) for z in range(nz)]
    ]
    circles = lax.all_to_all(
        grid_values, ("lev", "lat"), 0, 0, axis_index_groups=halves, tiled=True
    )
    circles = circles.reshape((levs, nc, half_bands // nc) + grid_values.shape[1:])

    steps = 2
    table = jnp.transpose(pair_table.reshape(levs, ny, nz, nc, slots), (0, 3, 1, 2, 4))
    table = table.reshape(steps, dev_count // steps, slots)
    other = top - table
    odd = table % 2 == 1
    kinds = []
    for wave in (jnp.where(odd, other, table), jnp.where(odd, table, other)):
        head = jnp.repeat(wave[:, :, : slots - 1], 2, axis=2).reshape(steps, -1)
        kinds.append(jnp.concatenate([head, wave[:, :, slots - 1], wave[:, :, slots - 1]], axis=1))
    waves = jnp.stack(kinds, axis=1)
    row = jnp.arange(waves.shape[2], dtype=jnp.int32)
    main = dev_count // steps * 2 * (slots - 1)
    quarters = jnp.where(row < main, row % 2, (row >= main + dev_count // steps).astype(jnp.int32))
    quarters = jnp.broadcast_to(quarters, waves.shape)
    lane = jnp.arange(LANES, dtype=jnp.int32)
    lane_index = jnp.broadcast_to(jnp.where(south == 1, LANES - 1 - lane, lane), (8, LANES))
    me = me_lev[None].astype(jnp.int32)
    pairs = lax.dynamic_slice_in_dim(pair_table, (me_lev * lat_count + me_lat) * slots, slots)
    rates = jnp.roll(damping_rates.reshape(levs, 1, group), -me_lev, axis=0)
    rates = jnp.broadcast_to(rates, (levs, 2, group)).reshape(-1, 1)
    rates = jnp.broadcast_to(rates, (rates.shape[0], LANES))
    spread = lambda v: jnp.broadcast_to(v.reshape(-1)[:, None], (v.size, LANES))
    wave_rows, quarter_rows, lane_index, south, me, pairs, rates = lax.optimization_barrier(
        (spread(waves), spread(quarters), lane_index, south[None], me, pairs, rates)
    )
    basis, last = turn(jnp.transpose(basis_table, (1, 2, 0)))
    circle = circle_table(wave_rows, quarter_rows, lon_count, lon_count // 2)
    circle = circle.reshape(waves.shape + (lon_count // 2,))
    packed = fourier(south, circles, circle, lane_index, dev_count)
    received = lax.all_to_all(
        packed, ("lev", "lat"), 0, 0, axis_index_groups=everyone, tiled=True
    ).reshape((levs, nc, ny, nz) + packed.shape[1:])
    parts, edges = [], []
    for first, count in CHUNKS:
        norm = float(top * (top + 1))
        x = gather(first, count, me, received, slots, lat_half)
        outs = legendre(first, count, pairs, x, basis, last, rates, edges, levs, lon_count, norm)
        edges = list(outs[levs:])
        moved = [outs[0]]
        for s in range(1, levs):
            to = [(i, (i + s) % levs) for i in range(levs)]
            moved.append(lax.ppermute(outs[s], "lev", to))
        parts.append(moved)
    for s in range(1, levs):
        edges[s] = lax.ppermute(edges[s], "lev", [(i, (i + s) % levs) for i in range(levs)])
    return assemble(me, parts, edges).reshape(slots, levs, 2, group, cols)


CHUNKS = ((0, 2), (2, 3))
LAT_AXES = (4, 4, 2)


def solution(mesh):
    placed = (P(None, "lat", "lev"), P(None, ("lev", "lat"), None), P(), P())
    return jax.shard_map(
        transform,
        mesh=mesh,
        in_specs=placed,
        out_specs=P("lat", None, None, "lev", None),
        check_vma=False,
    )
```

```python
import functools
import math

import jax
import jax.numpy as jnp
from jax import lax
from jax.experimental import pallas as pl
from jax.experimental.pallas import tpu as pltpu
from jax.sharding import PartitionSpec as P


F32 = jnp.float32
BF16 = jnp.bfloat16
NT = (((1,), (1,)), ((), ()))
NN = (((1,), (0,)), ((), ()))
LANES = 128


COS_TERMS = [((-1) ** n) * (2 * math.pi) ** (2 * n) / math.factorial(2 * n) for n in range(10)]


def cos_turns(turns):
    part = turns - jnp.floor(turns + 0.5)
    square = part * part
    total = jnp.full_like(square, COS_TERMS[-1])
    for term in COS_TERMS[-2::-1]:
        total = total * square + term
    return total


def circle_kernel(lon_count, wave_ref, quarter_ref, out_ref):
    rows, cols = out_ref.shape
    size = 64
    lane = lax.broadcasted_iota(jnp.int32, (size, LANES), 1).astype(F32)

    def block(i, carry):
        span = pl.ds(pl.multiple_of(i * size, size), size)
        wave = wave_ref[span, :].astype(F32)
        quarter = quarter_ref[span, :].astype(F32) * 0.25

        def turns(product):
            product = product - jnp.floor(product * (1.0 / lon_count)) * lon_count
            return product * (1.0 / lon_count)

        twice = 2.0 * cos_turns(turns(wave * float(LANES)))
        before = cos_turns(turns(wave * lane) + quarter)
        now = cos_turns(turns(wave * (lane + float(LANES))) + quarter)
        out_ref[span, :LANES] = before.astype(BF16)
        out_ref[span, LANES : 2 * LANES] = now.astype(BF16)
        for tile in range(2, cols // LANES):
            before, now = now, twice * now - before
            out_ref[span, tile * LANES : (tile + 1) * LANES] = now.astype(BF16)
        return carry

    lax.fori_loop(0, rows // size, block, 0)


def circle_table(waves, quarters, lon_count, cols):
    rows = waves.shape[0]
    return pl.pallas_call(
        functools.partial(circle_kernel, lon_count),
        in_specs=[VMEM_SPEC] * 2,
        out_specs=VMEM_SPEC,
        out_shape=jax.ShapeDtypeStruct((rows, cols), BF16),
        compiler_params=pltpu.CompilerParams(vmem_limit_bytes=CIRCLE_VMEM),
        cost_estimate=pl.CostEstimate(
            flops=rows * cols * 10, bytes_accessed=rows * cols * 2, transcendentals=0
        ),
        name="circle",
    )(waves, quarters)


VMEM_SPEC = pl.BlockSpec(memory_space=pltpu.VMEM)
HBM_SPEC = pl.BlockSpec(memory_space=pltpu.HBM)


def in_hbm(x):
    return pltpu.with_memory_space_constraint(x, pltpu.HBM)


CIRCLE_VMEM = 12 * 1024 * 1024


def fourier_kernel(
    south_ref, g_ref, table_ref, lane_ref, out_ref, circle_ref, fold_ref, tail_ref, sem
):
    _, cores, bands, lats, quarter = g_ref.shape
    bands = bands * cores
    steps = circle_ref.shape[0]
    tiles = bands * lats // LANES
    end = out_ref.shape[1] - tiles * 16
    dests = out_ref.shape[0] // steps
    main = dests * 8
    south = south_ref[0]

    def table_copy(i):
        return pltpu.make_async_copy(table_ref.at[i], circle_ref.at[i], sem.at[i])

    for i in range(steps):
        table_copy(i).start()
    tail_ref[...] = jnp.zeros_like(tail_ref)

    def fold(j, carry):
        def squared(q):
            value = g_ref[q, :, j].astype(F32)
            return (value * jnp.abs(value)).reshape(cores * lats, quarter)

        rows = pl.ds(pl.multiple_of(j * cores * lats, 16), cores * lats)
        for half in range(2):
            near, far = squared(half), squared(half + 2)
            cols = slice(half * quarter, (half + 1) * quarter)
            fold_ref[0, rows, cols] = (near + far).astype(BF16)
            fold_ref[1, rows, cols] = (near - far).astype(BF16)
        return carry

    lax.fori_loop(0, bands // cores, fold, 0)
    index = jnp.broadcast_to(lane_ref[0:1, :], (circle_ref.shape[2], LANES))

    def step(i, carry):
        table_copy(i).wait()
        span = pl.ds(i * dests, dests)
        for low in range(0, tiles, 2):
            many = min(2, tiles - low)
            rows = slice(low * LANES, (low + many) * LANES)
            values = [
                lax.dot_general(
                    circle_ref[i, kind], fold_ref[kind, rows, :], NT, preferred_element_type=F32
                )
                for kind in range(2)
            ]
            for at in range(many):
                place = jnp.where(south == 1, tiles - 1 - (low + at), low + at)
                both = []
                for kind in range(2):
                    value = jnp.take_along_axis(
                        values[kind][:, at * LANES : (at + 1) * LANES],
                        index,
                        axis=1,
                        mode="promise_in_bounds",
                    )
                    both.append(value[:main].reshape(dests, 8, LANES))
                    for r in range(2):
                        spot = pl.ds(place * 4 + kind * 2 + r, dests, stride=end)
                        tail_ref[spot, :] = value[main + r * dests : main + (r + 1) * dests]
                rows16 = pl.ds(pl.multiple_of(place * 16, 16), 16)
                out_ref[span, rows16, :] = jnp.concatenate(both, axis=1).astype(BF16)
        last = tail_ref[: dests * end].reshape(dests, end, LANES)
        out_ref[span, tiles * 16 :, :] = last.astype(BF16)
        return carry

    lax.fori_loop(0, steps, step, 0)


def fourier(south, received, circle, lane_index, dev_count):
    steps = circle.shape[0]
    dests = dev_count // steps
    _, cores, bands, lats, quarter = received.shape
    lat_half = cores * bands * lats
    tiles = lat_half // LANES
    end = -(-tiles * 4 // 8) * 8
    rows = tiles * 16 + end
    return pl.pallas_call(
        fourier_kernel,
        in_specs=[pl.BlockSpec(memory_space=pltpu.SMEM), VMEM_SPEC, HBM_SPEC, VMEM_SPEC],
        out_specs=VMEM_SPEC,
        scratch_shapes=[
            pltpu.VMEM(circle.shape, BF16),
            pltpu.VMEM((2, lat_half, 2 * quarter), BF16),
            pltpu.VMEM((dests * end + 8 * end, LANES), F32),
            pltpu.SemaphoreType.DMA((steps,)),
        ],
        out_shape=jax.ShapeDtypeStruct((dev_count, rows, LANES), BF16),
        compiler_params=pltpu.CompilerParams(vmem_limit_bytes=FOURIER_VMEM),
        cost_estimate=pl.CostEstimate(
            flops=2 * circle.size * lat_half,
            bytes_accessed=2 * (received.size + circle.size + dev_count * rows * LANES),
            transcendentals=0,
        ),
        name="fourier",
    )(south, received, in_hbm(circle), lane_index)


FOURIER_VMEM = 24 * 1024 * 1024
LEGENDRE_VMEM = 24 * 1024 * 1024


def gather_kernel(first, total, me_ref, recv_ref, x_ref, main_ref, tail_ref):
    levs, nc, ny, nz = recv_ref.shape[:4]
    group = nc * ny * nz // 2
    count, _, _, tiles, rows, _ = x_ref.shape
    mains = range(first, min(first + count, total - 1))
    end = recv_ref.shape[4] - tiles * 16
    part = rows // levs

    def step(x, carry):
        base = lax.rem(x - me_ref[0] + levs, levs) * part

        def sides(span, height, into):
            n = recv_ref[x, :, : ny // 2, :, span, :].astype(F32).reshape(group * height, LANES)
            s = recv_ref[x, :, ny // 2 :, :, span, :].astype(F32).reshape(group * height, LANES)
            into[0, : group * height] = n + s
            into[1, : group * height] = n - s

        def put(slot, kind, tile, r, from_ref, start, stride):
            dest = pl.ds(pl.multiple_of(base + r * group, 16), group)
            for par in range(2):
                value = from_ref[par, pl.ds(start, group, stride=stride), :]
                x_ref[slot - first, par, kind, tile, dest, :] = value.astype(BF16)

        for tile in range(tiles):
            sides(slice(tile * 16, tile * 16 + 16), 16, main_ref.at[tile])
            for kind in range(2):
                for k in mains:
                    for r in range(2):
                        put(k, kind, tile, r, main_ref.at[tile], kind * 8 + k * 2 + r, 16)
        if first + count == total:
            sides(slice(tiles * 16, tiles * 16 + end), end, tail_ref)
            for tile in range(tiles):
                for kind in range(2):
                    for r in range(2):
                        put(total - 1, kind, tile, r, tail_ref, tile * 4 + kind * 2 + r, end)
        return carry

    lax.fori_loop(0, levs, step, 0)


def turn_kernel(basis_ref, out_ref, last_ref):
    lats, waves = out_ref.shape[1:]
    size = 256
    row = lax.broadcasted_iota(jnp.int32, (size, size), 0)
    eye = (row == lax.broadcasted_iota(jnp.int32, (size, size), 1)).astype(BF16)
    for start in range(0, waves, size):
        for low in range(0, lats, size):
            high = min(low + size, lats)
            out_ref[0, low:high, start : start + size] = lax.dot_general(
                eye[: high - low, : high - low],
                basis_ref[0, start : start + size, low:high],
                NT,
                preferred_element_type=F32,
            ).astype(BF16)
    last_ref[0] = basis_ref[0, waves:, :]


def turn(basis):
    slots, cols, lats = basis.shape
    return pl.pallas_call(
        turn_kernel,
        grid=(slots,),
        in_specs=[pl.BlockSpec((1, cols, lats), lambda k: (k, 0, 0))],
        out_specs=[
            pl.BlockSpec((1, lats, cols - 1), lambda k: (k, 0, 0)),
            pl.BlockSpec((1, 1, lats), lambda k: (k, 0, 0)),
        ],
        out_shape=[
            jax.ShapeDtypeStruct((slots, lats, cols - 1), BF16),
            jax.ShapeDtypeStruct((slots, 1, lats), BF16),
        ],
        compiler_params=pltpu.CompilerParams(vmem_limit_bytes=LEGENDRE_VMEM),
        cost_estimate=pl.CostEstimate(
            flops=2 * 256 * basis.size, bytes_accessed=4 * basis.size, transcendentals=0
        ),
        name="turn",
    )(basis)


def gather(first, count, me, received, slots, lats):
    levs, nc, ny, nz, rows, _ = received.shape
    group = nc * ny * nz // 2
    tiles = lats // LANES
    end = rows - tiles * 16
    return pl.pallas_call(
        functools.partial(gather_kernel, first, slots),
        in_specs=[pl.BlockSpec(memory_space=pltpu.SMEM), VMEM_SPEC],
        out_specs=VMEM_SPEC,
        scratch_shapes=[
            pltpu.VMEM((tiles, 2, group * 16 + 128, LANES), F32),
            pltpu.VMEM((2, group * end + 8 * end, LANES), F32),
        ],
        out_shape=jax.ShapeDtypeStruct((count, 2, 2, tiles, levs * 2 * group, LANES), BF16),
        compiler_params=pltpu.CompilerParams(vmem_limit_bytes=LEGENDRE_VMEM),
        cost_estimate=pl.CostEstimate(
            flops=20 * received.size, bytes_accessed=4 * received.size, transcendentals=0
        ),
        name="gather",
    )(me, received)


def legendre_kernel(
    scale, norm, levs, first, count, pairs_ref, x_ref, basis_ref, last_ref, rate_ref, *refs
):
    out_refs, edge_refs = refs[-2 * levs : -levs], refs[-levs:]
    before = refs[: -2 * levs]
    waves = basis_ref.shape[2]
    tiles, rows = x_ref.shape[3:5]
    part = rows // levs
    width = 256
    rates = jnp.concatenate([rate_ref[...]] * (width // LANES), axis=1)

    def slot_step(k):
        pair = pairs_ref[k + first]
        bound = waves - pair
        first_kind = lax.rem(pair, 2)

        def damping(column, second):
            degree = jnp.where(second, column - 1, pair + column)
            scaled = (degree * (degree + 1)).astype(F32) / norm
            return scale / (1.0 + rates[:, : column.shape[1]] * (scaled * scaled))

        def side(par, kind):
            return jnp.concatenate([x_ref[k, par, kind, t] for t in range(tiles)], axis=1)

        def product(start, kind):
            column = start + lax.broadcasted_iota(jnp.int32, (1, width), 1)
            second = column >= bound
            even = lax.rem(jnp.where(second, column + pair, column), 2) == 0
            left = jnp.concatenate([side(0, kind), side(1, kind)], axis=0)
            basis = basis_ref[k + first, :, pl.ds(start, width)]
            both = lax.dot_general(left, basis, NN, preferred_element_type=F32)
            value = jnp.where(even, both[:rows], both[rows:]) * damping(column, second)
            return value.astype(BF16), second

        for start in range(0, waves, width):
            value, _ = product(start, jnp.where(start >= bound, 1 - first_kind, first_kind))
            for s in range(levs):
                out_refs[s][k, :, start : start + width] = value[s * part : (s + 1) * part]
        start = pl.multiple_of(jnp.minimum(bound // width, waves // width - 1) * width, width)
        value, second = product(start, 1 - first_kind)
        for s in range(levs):
            spot = (k, slice(None), pl.ds(start, width))
            kept = jnp.where(second, value[s * part : (s + 1) * part].astype(F32), out_refs[s][spot].astype(F32))
            out_refs[s][spot] = kept.astype(BF16)
        column = jnp.full((1, 1), waves, jnp.int32)
        left = side(first_kind, 1 - first_kind).astype(F32)
        final = jnp.sum(left * last_ref[k + first].astype(F32), axis=1, keepdims=True)
        return final * damping(column, column >= bound)

    lane = lax.broadcasted_iota(jnp.int32, (rows, LANES), 1)
    edge = jnp.zeros((rows, LANES), F32)
    if before:
        edge = jnp.concatenate([b[...].astype(F32) for b in before], axis=0)
    for k in range(count):
        edge = jnp.where(lane == k + first, slot_step(k), edge)
    for s in range(levs):
        edge_refs[s][...] = edge[s * part : (s + 1) * part].astype(BF16)


def legendre(first, count, pairs, x, basis, last, rates, before, levs, lon_count, norm):
    _, lats, waves = basis.shape
    cols = waves
    part = x.shape[4] // levs
    return pl.pallas_call(
        functools.partial(legendre_kernel, 1.0 / lon_count, norm, levs, first, count),
        in_specs=[pl.BlockSpec(memory_space=pltpu.SMEM)] + [VMEM_SPEC] * (4 + len(before)),
        out_specs=[VMEM_SPEC] * (2 * levs),
        out_shape=[jax.ShapeDtypeStruct((count, part, cols), BF16)] * levs
        + [jax.ShapeDtypeStruct((part, LANES), BF16)] * levs,
        compiler_params=pltpu.CompilerParams(vmem_limit_bytes=LEGENDRE_VMEM),
        cost_estimate=pl.CostEstimate(
            flops=2 * count * cols * lats * 256,
            bytes_accessed=2 * count * cols * (lats + 128),
            transcendentals=0,
        ),
        name="legendre",
    )(pairs, x, basis, last, rates, *before)


def assemble_kernel(counts, me_ref, *refs):
    out_ref = refs[-1]
    slots, levs, _, cols = out_ref.shape
    for s in range(levs):
        lev = lax.rem(me_ref[0] - s + levs, levs)
        low = 0
        for c, count in enumerate(counts):
            for k in range(count):
                out_ref[low + k, lev, :, : cols - 1] = refs[c * levs + s][k]
            low += count
        edge = refs[len(counts) * levs + s][...]
        for k in range(slots):
            out_ref[k, lev, :, cols - 1 :] = edge[:, k : k + 1]


def assemble(me, parts, edges):
    levs = len(edges)
    _, part, waves = parts[0][0].shape
    counts = [p[0].shape[0] for p in parts]
    flat = [a for p in parts for a in p] + edges
    return pl.pallas_call(
        functools.partial(assemble_kernel, counts),
        in_specs=[pl.BlockSpec(memory_space=pltpu.SMEM)] + [VMEM_SPEC] * len(flat),
        out_specs=VMEM_SPEC,
        out_shape=jax.ShapeDtypeStruct((sum(counts), levs, part, waves + 1), BF16),
        compiler_params=pltpu.CompilerParams(vmem_limit_bytes=LEGENDRE_VMEM),
        name="assemble",
    )(me, *flat)


def transform(grid_values, basis_table, damping_rates, pair_table):
    levs, lat_count = lax.axis_size("lev"), lax.axis_size("lat")
    dev_count = levs * lat_count
    half_bands = lat_count // 2
    lon_count = grid_values.shape[2] * levs
    slots, cols = basis_table.shape[1], basis_table.shape[2]
    top = cols - 2
    lat_half = basis_table.shape[0]
    group = half_bands
    me_lev, me_lat = lax.axis_index("lev"), lax.axis_index("lat")
    south = (me_lat >= half_bands).astype(jnp.int32)

    ny, nz, nc = LAT_AXES
    at = lambda x, y, z, c: x * lat_count + (y * nz + z) * nc + c
    halves = [
        [
            at(x, y + h * ny // 2, z, c)
            for x in range(levs)
            for c in range(nc)
            for y in range(ny // 2)
            for z in range(nz)
        ]
        for h in range(2)
    ]
    everyone = [
        [at(x, y, z, c) for x in range(levs) for c in range(nc) for y in range(ny) for z in range(nz)]
    ]
    circles = lax.all_to_all(
        grid_values, ("lev", "lat"), 0, 0, axis_index_groups=halves, tiled=True
    )
    circles = circles.reshape((levs, nc, half_bands // nc) + grid_values.shape[1:])

    steps = 2
    table = jnp.transpose(pair_table.reshape(levs, ny, nz, nc, slots), (0, 3, 1, 2, 4))
    table = table.reshape(steps, dev_count // steps, slots)
    other = top - table
    odd = table % 2 == 1
    kinds = []
    for wave in (jnp.where(odd, other, table), jnp.where(odd, table, other)):
        head = jnp.repeat(wave[:, :, : slots - 1], 2, axis=2).reshape(steps, -1)
        kinds.append(jnp.concatenate([head, wave[:, :, slots - 1], wave[:, :, slots - 1]], axis=1))
    waves = jnp.stack(kinds, axis=1)
    row = jnp.arange(waves.shape[2], dtype=jnp.int32)
    main = dev_count // steps * 2 * (slots - 1)
    quarters = jnp.where(row < main, row % 2, (row >= main + dev_count // steps).astype(jnp.int32))
    quarters = jnp.broadcast_to(quarters, waves.shape)
    lane = jnp.arange(LANES, dtype=jnp.int32)
    lane_index = jnp.broadcast_to(jnp.where(south == 1, LANES - 1 - lane, lane), (8, LANES))
    me = me_lev[None].astype(jnp.int32)
    pairs = lax.dynamic_slice_in_dim(pair_table, (me_lev * lat_count + me_lat) * slots, slots)
    rates = jnp.roll(damping_rates.reshape(levs, 1, group), -me_lev, axis=0)
    rates = jnp.broadcast_to(rates, (levs, 2, group)).reshape(-1, 1)
    rates = jnp.broadcast_to(rates, (rates.shape[0], LANES))
    spread = lambda v: jnp.broadcast_to(v.reshape(-1)[:, None], (v.size, LANES))
    wave_rows, quarter_rows, lane_index, south, me, pairs, rates = lax.optimization_barrier(
        (spread(waves), spread(quarters), lane_index, south[None], me, pairs, rates)
    )
    basis, last = turn(jnp.transpose(basis_table, (1, 2, 0)))
    circle = circle_table(wave_rows, quarter_rows, lon_count, lon_count // 2)
    circle = circle.reshape(waves.shape + (lon_count // 2,))
    packed = fourier(south, circles, circle, lane_index, dev_count)
    received = lax.all_to_all(
        packed, ("lev", "lat"), 0, 0, axis_index_groups=everyone, tiled=True
    ).reshape((levs, nc, ny, nz) + packed.shape[1:])
    parts, edges = [], []
    for first, count in CHUNKS:
        norm = float(top * (top + 1))
        x = gather(first, count, me, received, slots, lat_half)
        outs = legendre(first, count, pairs, x, basis, last, rates, edges, levs, lon_count, norm)
        edges = list(outs[levs:])
        moved = [outs[0]]
        for s in range(1, levs):
            to = [(i, (i + s) % levs) for i in range(levs)]
            moved.append(lax.ppermute(outs[s], "lev", to))
        parts.append(moved)
    for s in range(1, levs):
        edges[s] = lax.ppermute(edges[s], "lev", [(i, (i + s) % levs) for i in range(levs)])
    return assemble(me, parts, edges).reshape(slots, levs, 2, group, cols)


CHUNKS = ((0, 2), (2, 3))
LAT_AXES = (4, 4, 2)


def solution(mesh):
    placed = (P(None, "lat", "lev"), P(None, ("lev", "lat"), None), P(), P())
    return jax.shard_map(
        transform,
        mesh=mesh,
        in_specs=placed,
        out_specs=P("lat", None, None, "lev", None),
        check_vma=False,
    )
```
